256 devices in a mesh: dp: 128 (over z, x_lo, y, core), tensor: 2 (over x_hi).
Axes of the slice: x: 4 (x_hi: 2, x_lo: 2; x = x_hi * 2 + x_lo), y: 4, z: 8, core: 2. Of those that a mesh axis runs over, the one named last changes fastest.
Arguments:
- looked: bfloat16 [8192, 16384], P(('dp', 'tensor')), may hold values from -6 to 6
- column_owner: int32 [8192], replicated, may hold values from 0 to 8191, each once
- v_proj: bfloat16 [384, 8192], P(None, 'tensor'), may hold values from -0.0625 to 0.0625
- u_proj: bfloat16 [384, 8192], P(None, 'tensor'), may hold values from -0.3125 to 0.3125
- bias: float32 [8192], P('tensor'), may hold values from -3 to 3
- upstream: bfloat16 [8192, 16384], P('tensor', 'dp'), may hold values from -6 to 6
Outputs:
- d_looked: bfloat16 [8192, 16384], P(('dp', 'tensor'))
- grad_u: float32 [384, 8192], P('dp', 'tensor')
- grad_v: float32 [384, 8192], P('dp', 'tensor')
- grad_bias: float32 [8192], P('tensor')
The draws below stay inside these ranges and needn't reach their ends.
Inputs may be any that keep to these rules, and one draw needn't show every extreme that they name: A permutation of the 8192 feature columns: wire row r carries column column_owner[r].
All inputs are finite; a program needn't handle non-finite values.
Results may differ from the reference program's by a relative error of at most 0.0049.
Values may be sent and summed in bfloat16 or wider, within the bound.
No kernel may reach another device: no remote copies, remote signals or barrier semaphores. Data moves between devices by JAX's collectives and lax.ppermute only.
A program may use at most 128 MiB of HBM per device.

```python
import math
import jax
import jax.numpy as jnp
from jax import lax

R = 384
B_DEV = 128
W = 8192
SAMPLES = 16384
N_DP = 128


def shard_levels(rng, shape, shards, low, largest):
    def one(dim, parts):
        heights = jax.random.uniform(jax.random.fold_in(jax.random.fold_in(rng, 6), dim), (parts,), jnp.float32, low / len(shards), largest / len(shards))
        return jnp.repeat(jnp.exp(heights), shape[dim] // parts).reshape((-1,) + (1,) * (len(shape) - dim - 1))

    factor_of = one(*shards[0])
    for cut in shards[1:]:
        factor_of = factor_of * one(*cut)
    return factor_of


def normal_values(key, shape, width, reach, cuts=(), kind=jnp.bfloat16):
    array = jax.random.normal(key, shape, jnp.float32) * width
    if len(cuts) > 0:
        array = shard_levels(key, shape, cuts, -0.22, 0.18) * array
    return jnp.clip(array, min=-reach, max=reach).astype(kind)


def setup_inputs(seed: int = 0) -> dict:
    seeds = jax.random.split(jax.random.key(seed), 7)
    return {
        "looked": normal_values(seeds[0], (W, SAMPLES), 1.0, 6.0, ((0, 256),)),
        "column_owner": jax.random.permutation(seeds[1], W).astype(jnp.int32),
        "v_proj": normal_values(seeds[2], (R, W), W ** -0.5, 0.0625, ((1, 2),)),
        "u_proj": normal_values(seeds[3], (R, W), R ** -0.5, 0.3125, ((1, 2),)),
        "bias": normal_values(seeds[4], (W,), 0.5, 3.0, ((0, 2),), jnp.float32),
        "upstream": normal_values(seeds[5], (W, SAMPLES), 1.0, 6.0, ((0, 2), (1, 128))),
    }


def reference(looked, column_owner, v_proj, u_proj, bias, upstream):
    norm = 1.0 / math.sqrt(SAMPLES)
    x_full = jnp.zeros_like(looked).at[column_owner].set(looked)
    group = min(N_DP, 16)
    block_size = B_DEV * group
    blocks = SAMPLES // block_size
    grad_u = jnp.zeros((R, W), jnp.float32)
    grad_v = jnp.zeros((R, W), jnp.float32)
    grad_bias = jnp.zeros((W,), jnp.float32)
    pieces = []
    for index in range(blocks):
        x_zero = x_full[:, index * block_size:(index + 1) * block_size]
        cotan = upstream[:, index * block_size:(index + 1) * block_size].astype(jnp.float32)
        hrank = jnp.dot(v_proj, x_zero, preferred_element_type=jnp.float32).astype(jnp.bfloat16)
        mix = jnp.dot(u_proj.T, hrank, preferred_element_type=jnp.float32) + bias[:, None]
        scaled = cotan * x_zero.astype(jnp.float32)
        scaled16 = scaled.astype(jnp.bfloat16)
        grad_bias = grad_bias + lax.optimization_barrier(jnp.sum(scaled, axis=1))
        grad_u = grad_u + jnp.dot(hrank, scaled16.T, preferred_element_type=jnp.float32)
        dhrank = jnp.dot(u_proj, scaled16, preferred_element_type=jnp.float32).astype(jnp.bfloat16)
        grad_v = grad_v + jnp.dot(dhrank, x_zero.T, preferred_element_type=jnp.float32)
        dx_zero = cotan * (mix + 1.0) + jnp.dot(v_proj.T, dhrank, preferred_element_type=jnp.float32)
        pieces.append(dx_zero.astype(jnp.bfloat16))
    dx_full = jnp.concatenate(pieces, axis=1)
    d_looked = jnp.take(dx_full, column_owner, axis=0)
    return (d_looked, grad_u * norm, grad_v * norm, grad_bias * norm)
```

```python
import math

import jax
import jax.numpy as jnp
from jax import lax
from jax.sharding import Mesh, PartitionSpec as P

DP = ("z", "xl", "y", "c")
SWAP = [(0, 1), (1, 0)]


def dot_last(left, right):
    return lax.dot_general(
        left, right, (((1,), (1,)), ((), ())), preferred_element_type=jnp.float32
    )


def dot_first(left, right):
    return lax.dot_general(
        left, right, (((0,), (0,)), ((), ())), preferred_element_type=jnp.float32
    )


def shift(value, axis, size, by):
    return lax.ppermute(value, axis, [(i, (i + by) % size) for i in range(size)])


def split3(value):
    high = lax.reduce_precision(value, 8, 7)
    rest = value - high
    middle = lax.reduce_precision(rest, 8, 7)
    parts = jnp.concatenate([high, middle, rest - middle], axis=0)
    return parts.astype(jnp.bfloat16)


def join3(parts):
    rows = parts.shape[0] // 3
    wide = parts.astype(jnp.float32)
    return wide[:rows] + wide[rows : 2 * rows] + wide[2 * rows :]


def take_rows(table, rows):
    return table.at[rows].get(mode="promise_in_bounds", unique_indices=True)


def inverse_rows(column_owner, first_column, count):
    wires = jnp.arange(column_owner.shape[0], dtype=jnp.int32)
    high = column_owner // 128 - first_column // 128
    low = column_owner % 128
    pick = (high[None, :] == jnp.arange(count // 128, dtype=jnp.int32)[:, None]).astype(jnp.bfloat16)
    lanes = low[:, None] == jnp.arange(128, dtype=jnp.int32)[None, :]
    values = jnp.concatenate(
        [
            jnp.where(lanes, (wires // 128)[:, None].astype(jnp.bfloat16), 0),
            jnp.where(lanes, (wires % 128)[:, None].astype(jnp.bfloat16), 0),
        ],
        axis=1,
    )
    found = jnp.dot(pick, values, preferred_element_type=jnp.float32).astype(jnp.int32)
    return (found[:, :128] * 128 + found[:, 128:]).reshape(-1)


def per_device(looked, column_owner, v_proj, u_proj, bias, upstream):
    z, xl, y, c, t = (lax.axis_index(a) for a in DP + ("t",))
    nz, ny = lax.axis_size("z"), lax.axis_size("y")
    dp_count = lax.axis_size(DP)
    block_rows = looked.shape[0]
    rank, half_width = v_proj.shape
    samples = upstream.shape[1]
    norm = 1.0 / math.sqrt(samples * dp_count)
    bf16 = jnp.bfloat16

    arrived = lax.all_to_all(looked, DP, split_axis=1, concat_axis=0, tiled=True)
    partner = lax.ppermute(arrived, "t", SWAP)
    wire = inverse_rows(column_owner, t * half_width, half_width)
    side = wire // block_rows % 2
    place = wire // (2 * block_rows) * block_rows + wire % block_rows
    x_rows = jnp.where(side == t, 0, half_width) + place
    x_zero = take_rows(jnp.concatenate([arrived, partner], axis=0), x_rows)

    cotan = upstream.astype(jnp.float32)
    scaled = cotan * x_zero.astype(jnp.float32)
    scaled16 = scaled.astype(bf16)
    bias_part = jnp.sum(scaled, axis=1).reshape(-1, 128)
    part = jnp.concatenate(
        [
            jnp.dot(v_proj, x_zero, preferred_element_type=jnp.float32),
            jnp.dot(u_proj, scaled16, preferred_element_type=jnp.float32),
        ],
        axis=0,
    )
    ranks = (part + lax.ppermute(part, "t", SWAP)).astype(bf16)
    hrank, dhrank = ranks[:rank], ranks[rank:]

    wide = half_width // (2 * ny)
    both = jnp.stack([x_zero, scaled16]).reshape(2, ny, 2, wide, samples)
    kept = lax.dynamic_index_in_dim(both, c, 2, keepdims=False)
    given = lax.ppermute(lax.dynamic_index_in_dim(both, 1 - c, 2, keepdims=False), "c", SWAP)
    chip = jnp.stack([kept, given])
    blocks = [lax.dynamic_index_in_dim(chip, y, 2, keepdims=False)]
    for k in range(1, ny):
        block = lax.dynamic_index_in_dim(chip, (y + k) % ny, 2, keepdims=False)
        blocks.append(shift(block, "y", ny, k))

    bias_rows = bias_part.shape[0]
    message = jnp.concatenate([ranks, split3(bias_part)], axis=0)
    rank_blocks = [ranks]
    for k in range(1, ny):
        got = shift(message, "y", ny, k)
        rank_blocks.append(got[: 2 * rank])
        bias_part = bias_part + join3(got[2 * rank :])
    message = jnp.concatenate(rank_blocks + [split3(bias_part)], axis=0)
    got = lax.ppermute(message, "c", SWAP)
    bias_part = bias_part + join3(got[2 * rank * ny :])
    rank_all = jnp.concatenate(
        rank_blocks + [got[2 * rank * k : 2 * rank * (k + 1)] for k in range(ny)], axis=1
    )
    x_all = jnp.concatenate([b[i, 0] for i in range(2) for b in blocks], axis=1)
    s_all = jnp.concatenate([b[i, 1] for i in range(2) for b in blocks], axis=1)
    grads = jnp.concatenate(
        [dot_last(rank_all[:rank], s_all), dot_last(rank_all[rank:], x_all)], axis=1
    )

    z_rows = rank // nz
    grads16 = grads.astype(bf16)
    bias3 = split3(bias_part).reshape(-1, 2 * wide)
    total = lax.dynamic_slice_in_dim(grads, z * z_rows, z_rows)
    for k in range(1, nz):
        piece = lax.dynamic_slice_in_dim(grads16, (z + k) % nz * z_rows, z_rows)
        got = shift(jnp.concatenate([piece, bias3], axis=0), "z", nz, k)
        total = total + got[:z_rows].astype(jnp.float32)
        bias_part = bias_part + join3(got[z_rows:].reshape(-1, 128))
    halves = total.reshape(2, z_rows // 2, 2 * wide)
    bias_piece = bias_part.reshape(-1, 2 * wide)
    message = jnp.concatenate(
        [lax.dynamic_index_in_dim(halves, 1 - xl, 0, keepdims=False), bias_piece], axis=0
    )
    got = lax.ppermute(message, "xl", SWAP)
    total = lax.dynamic_index_in_dim(halves, xl, 0, keepdims=False) + got[: z_rows // 2]
    grad_bias = (bias_piece + got[z_rows // 2 :]).reshape(-1) * norm
    group = 2 * ny
    total = lax.all_to_all(
        (total * norm).reshape(group, -1, 2 * wide), ("y", "c"), split_axis=0, concat_axis=0, tiled=True
    )
    total = total.reshape(group, -1, 2, wide).transpose(2, 1, 0, 3).reshape(2, -1, half_width)

    mix = dot_first(u_proj, hrank) + bias[:, None]
    dx_zero = (cotan * (mix + 1.0) + dot_first(v_proj, dhrank)).astype(bf16)
    dx_other = lax.ppermute(dx_zero, "t", SWAP)
    columns = lax.dynamic_index_in_dim(
        column_owner.reshape(dp_count, 2, block_rows), t, 1, keepdims=False
    ).reshape(-1)
    out_rows = jnp.where(columns // half_width == t, 0, half_width) + columns % half_width
    outgoing = take_rows(jnp.concatenate([dx_zero, dx_other], axis=0), out_rows)
    d_looked = lax.all_to_all(outgoing, DP, split_axis=0, concat_axis=1, tiled=True)
    return (d_looked, total[0], total[1], grad_bias)


def solution(mesh):
    fine = Mesh(mesh.devices.reshape(8, 2, 4, 2, 2), DP + ("t",))
    in_specs = (
        P(DP + ("t",), None),
        P(),
        P(None, "t"),
        P(None, "t"),
        P("t"),
        P("t", DP),
    )
    out_specs = (P(DP + ("t",), None), P(DP, "t"), P(DP, "t"), P("t"))
    return jax.shard_map(
        per_device, mesh=fine, in_specs=in_specs, out_specs=out_specs, check_vma=False
    )
```

```python
import math

import jax
import jax.numpy as jnp
from jax import lax
from jax.experimental import pallas as pl
from jax.experimental.pallas import tpu as pltpu
from jax.sharding import Mesh, PartitionSpec as P

DP = ("z", "xl", "y", "c")
SWAP = [(0, 1), (1, 0)]
UNROLL = 32
SMEM = pl.BlockSpec(memory_space=pltpu.SMEM)
VMEM = pl.BlockSpec(memory_space=pltpu.VMEM)


def dot_last(left, right, precision=None):
    return lax.dot_general(
        left, right, (((1,), (1,)), ((), ())), precision=precision, preferred_element_type=jnp.float32
    )


def dot_first(left, right):
    return lax.dot_general(
        left, right, (((0,), (0,)), ((), ())), preferred_element_type=jnp.float32
    )


def shift(value, axis, size, by):
    return lax.ppermute(value, axis, [(i, (i + by) % size) for i in range(size)])


def split3(value):
    high = lax.reduce_precision(value, 8, 7)
    rest = value - high
    middle = lax.reduce_precision(rest, 8, 7)
    parts = jnp.concatenate([high, middle, rest - middle, jnp.zeros_like(value)], axis=0)
    return parts.astype(jnp.bfloat16)


def join3(parts):
    rows = parts.shape[0] // 4
    wide = parts.astype(jnp.float32)
    return wide[:rows] + wide[rows : 2 * rows] + wide[2 * rows : 3 * rows]


def pick_rows(rows, table, picked):
    def step(i, carry):
        for j in range(UNROLL):
            k = i * UNROLL + j
            picked[pl.ds(k, 1), :] = table[pl.ds(rows[k], 1), :]
        return carry

    lax.fori_loop(0, picked.shape[0] // UNROLL, step, 0)


def gather_kernel(rows, near, far, out, table, picked):
    half = near.shape[0]
    table[:half] = near[...].astype(jnp.float32)
    table[half:] = far[...].astype(jnp.float32)
    pick_rows(rows, table, picked)
    out[...] = picked[...].astype(out.dtype)


def gather(rows, near, far):
    count, lanes = rows.shape[0], near.shape[1]
    return pl.pallas_call(
        gather_kernel,
        out_shape=jax.ShapeDtypeStruct((count, lanes), near.dtype),
        in_specs=[SMEM, VMEM, VMEM],
        out_specs=VMEM,
        scratch_shapes=[
            pltpu.VMEM((2 * near.shape[0], lanes), jnp.float32),
            pltpu.VMEM((count, lanes), jnp.float32),
        ],
        compiler_params=pltpu.CompilerParams(vmem_limit_bytes=24 * 2**20),
        name="gather_rows",
    )(rows, near, far)


def forward_kernel(place, rows, near, far, upstream, v_proj, u_proj, *rest):
    groups, (part, bias_out, table, picked) = rest[:-4], rest[-4:]
    half = near.shape[0]
    rank = v_proj.shape[0]
    ny = len(groups)
    wide = groups[0].shape[2]
    table[:half] = near[...].astype(jnp.float32)
    table[half:] = far[...].astype(jnp.float32)
    pick_rows(rows, table, picked)
    y, c = place[0], place[1]
    ones = jnp.ones((8, near.shape[1]), jnp.float32)
    part[...] = jnp.zeros_like(part)
    for k in range(ny):
        for i in range(2):
            block = lax.rem(y + k, ny) * 2 + (c + i - 2 * c * i)
            start = pl.multiple_of(block * wide, wide)
            x = picked[pl.ds(start, wide), :]
            scaled = upstream[pl.ds(start, wide), :].astype(jnp.float32) * x
            x16 = x.astype(jnp.bfloat16)
            s16 = scaled.astype(jnp.bfloat16)
            groups[k][i, 0] = x16
            groups[k][i, 1] = s16
            sums = dot_last(ones, scaled, lax.Precision.HIGHEST)
            bias_out[pl.ds(block, 1), :] = sums[:1]
            part[:rank] += jnp.dot(
                v_proj[:, pl.ds(start, wide)], x16, preferred_element_type=jnp.float32
            )
            part[rank:] += jnp.dot(
                u_proj[:, pl.ds(start, wide)], s16, preferred_element_type=jnp.float32
            )


def forward(place, rows, near, far, upstream, v_proj, u_proj, ny):
    half, lanes = near.shape
    rank = v_proj.shape[0]
    wide = half // (2 * ny)
    group = jax.ShapeDtypeStruct((2, 2, wide, lanes), jnp.bfloat16)
    return pl.pallas_call(
        forward_kernel,
        out_shape=[group] * ny
        + [
            jax.ShapeDtypeStruct((2 * rank, lanes), jnp.float32),
            jax.ShapeDtypeStruct((2 * ny, wide), jnp.float32),
        ],
        in_specs=[SMEM, SMEM] + [VMEM] * 5,
        out_specs=[VMEM] * (ny + 2),
        scratch_shapes=[
            pltpu.VMEM((2 * half, lanes), jnp.float32),
            pltpu.VMEM((half, lanes), jnp.float32),
        ],
        compiler_params=pltpu.CompilerParams(vmem_limit_bytes=40 * 2**20),
        name="gather_and_project",
    )(place, rows, near, far, upstream, v_proj, u_proj)


def grads_kernel(place, bias3, *rest, ny, nz, rank):
    ranks, far_ranks = rest[:ny], rest[ny]
    groups, far_group = rest[ny + 1 : 2 * ny + 1], rest[2 * ny + 1]
    own, *pieces, result = rest[2 * ny + 2 :]
    wide = far_group.shape[2]
    rows = rank // nz
    for part in range(2):
        lo = part * rank
        acc = jnp.zeros((rank, wide), jnp.float32)
        for k in range(ny):
            left = jnp.concatenate(
                [
                    ranks[k][lo : lo + rank, :],
                    far_ranks[k * 2 * rank + lo : k * 2 * rank + lo + rank, :],
                ],
                axis=1,
            )
            right = jnp.concatenate([groups[k][0, 1 - part], far_group[k, 1 - part]], axis=1)
            acc = acc + dot_last(left, right)
        result[:, part * wide : (part + 1) * wide] = acc
    z = place[0]
    own[...] = result[pl.ds(pl.multiple_of(z * rows, 16), rows), :]
    extra = pieces[0].shape[0] - rows
    for k, piece in enumerate(pieces, 1):
        first = pl.multiple_of(lax.rem(z + k, nz) * rows, 16)
        piece[:rows, :] = result[pl.ds(first, rows), :].astype(jnp.bfloat16)
        for j in range(2 * wide // 128):
            piece[rows:, j * 128 : (j + 1) * 128] = bias3[j * extra : (j + 1) * extra, :]


def gradients(place, bias3, ranks, far_ranks, groups, far_group, nz, rank):
    ny, wide = len(groups), far_group.shape[2]
    rows = rank // nz
    extra = bias3.shape[0] * 128 // (2 * wide)
    body = lambda *refs: grads_kernel(*refs, ny=ny, nz=nz, rank=rank)
    return pl.pallas_call(
        body,
        out_shape=[jax.ShapeDtypeStruct((rows, 2 * wide), jnp.float32)]
        + [jax.ShapeDtypeStruct((rows + extra, 2 * wide), jnp.bfloat16)] * (nz - 1),
        in_specs=[SMEM] + [VMEM] * (2 * ny + 3),
        out_specs=[VMEM] * nz,
        scratch_shapes=[pltpu.VMEM((rank, 2 * wide), jnp.float32)],
        compiler_params=pltpu.CompilerParams(vmem_limit_bytes=32 * 2**20),
        name="regrouped_grads",
    )(place, bias3, *ranks, far_ranks, *groups, far_group)


def inverse_rows(column_owner, first_column, count):
    wires = jnp.arange(column_owner.shape[0], dtype=jnp.int32)
    high = column_owner // 128 - first_column // 128
    low = column_owner % 128
    pick = (high[None, :] == jnp.arange(count // 128, dtype=jnp.int32)[:, None]).astype(jnp.bfloat16)
    lanes = low[:, None] == jnp.arange(128, dtype=jnp.int32)[None, :]
    values = jnp.concatenate(
        [
            jnp.where(lanes, (wires // 128)[:, None].astype(jnp.bfloat16), 0),
            jnp.where(lanes, (wires % 128)[:, None].astype(jnp.bfloat16), 0),
        ],
        axis=1,
    )
    found = jnp.dot(pick, values, preferred_element_type=jnp.float32).astype(jnp.int32)
    return (found[:, :128] * 128 + found[:, 128:]).reshape(-1)


def per_device(looked, column_owner, v_proj, u_proj, bias, upstream):
    z, xl, y, c, t = (lax.axis_index(a) for a in DP + ("t",))
    nz, ny = lax.axis_size("z"), lax.axis_size("y")
    dp_count = lax.axis_size(DP)
    block_rows = looked.shape[0]
    rank, half_width = v_proj.shape
    samples = upstream.shape[1]
    norm = 1.0 / math.sqrt(samples * dp_count)
    bf16 = jnp.bfloat16

    arrived = lax.all_to_all(looked, DP, split_axis=1, concat_axis=0, tiled=True)
    partner = lax.ppermute(arrived, "t", SWAP)
    wire = inverse_rows(column_owner, t * half_width, half_width)
    side = wire // block_rows % 2
    spot = wire // (2 * block_rows) * block_rows + wire % block_rows
    x_rows = jnp.where(side == t, 0, half_width) + spot
    *groups, part, bias_part = forward(
        jnp.stack([y, c]).astype(jnp.int32), x_rows, arrived, partner, upstream, v_proj, u_proj, ny
    )
    ranks = (part + lax.ppermute(part, "t", SWAP)).astype(bf16)
    hrank, dhrank = ranks[:rank], ranks[rank:]

    mix = dot_first(u_proj, hrank) + bias[:, None]
    cotan = upstream.astype(jnp.float32)
    dx_zero = (cotan * (mix + 1.0) + dot_first(v_proj, dhrank)).astype(bf16)
    dx_other = lax.ppermute(dx_zero, "t", SWAP)

    groups = [groups[0]] + [shift(groups[k], "y", ny, k) for k in range(1, ny)]
    far_group = lax.ppermute(jnp.stack([g[1] for g in groups]), "c", SWAP)
    bias_part = bias_part.reshape(-1, 128)
    message = jnp.concatenate([ranks, split3(bias_part)], axis=0)
    message, _ = lax.optimization_barrier((message, dx_zero))
    rank_blocks = [ranks]
    for k in range(1, ny):
        got = shift(message, "y", ny, k)
        rank_blocks.append(got)
        bias_part = bias_part + join3(got[2 * rank :])
    message = jnp.concatenate([b[: 2 * rank] for b in rank_blocks] + [split3(bias_part)], axis=0)
    far_ranks = lax.ppermute(message, "c", SWAP)
    bias_part = bias_part + join3(far_ranks[2 * rank * ny :])
    total, *pieces = gradients(
        z.astype(jnp.int32)[None], split3(bias_part), rank_blocks, far_ranks, groups, far_group, nz, rank
    )
    pieces = [shift(p, "z", nz, k) for k, p in enumerate(pieces, 1)]

    columns = lax.dynamic_index_in_dim(
        column_owner.reshape(dp_count, 2, block_rows), t, 1, keepdims=False
    ).reshape(-1)
    out_rows = jnp.where(columns // half_width == t, 0, half_width) + columns % half_width
    outgoing = gather(out_rows, dx_zero, dx_other)
    d_looked = lax.all_to_all(outgoing, DP, split_axis=0, concat_axis=1, tiled=True)

    pieces, _ = lax.optimization_barrier((pieces, outgoing))
    z_rows = rank // nz
    wide = total.shape[1]
    extra = pieces[0].shape[0] - z_rows
    total = total + sum(p[:z_rows].astype(jnp.float32) for p in pieces)
    spread = lambda p: p.reshape(extra, wide // 128, 128).transpose(1, 0, 2).reshape(-1, 128)
    bias_part = bias_part + sum(join3(spread(p[z_rows:])) for p in pieces)
    halves = total.reshape(2, z_rows // 2, wide)
    bias_piece = bias_part.reshape(-1, wide)
    message = jnp.concatenate(
        [lax.dynamic_index_in_dim(halves, 1 - xl, 0, keepdims=False), bias_piece], axis=0
    )
    got = lax.ppermute(message, "xl", SWAP)
    total = lax.dynamic_index_in_dim(halves, xl, 0, keepdims=False) + got[: z_rows // 2]
    grad_bias = (bias_piece + got[z_rows // 2 :]).reshape(-1) * norm
    total = lax.all_to_all(
        (total * norm).reshape(2 * ny, -1, wide), ("y", "c"), split_axis=0, concat_axis=0, tiled=True
    )
    total = total.reshape(2 * ny, -1, 2, wide // 2).transpose(2, 1, 0, 3).reshape(2, -1, half_width)
    return (d_looked, total[0], total[1], grad_bias)


def solution(mesh):
    fine = Mesh(mesh.devices.reshape(8, 2, 4, 2, 2), DP + ("t",))
    in_specs = (
        P(DP + ("t",), None),
        P(),
        P(None, "t"),
        P(None, "t"),
        P("t"),
        P("t", DP),
    )
    out_specs = (P(DP + ("t",), None), P(DP, "t"), P(DP, "t"), P("t"))
    return jax.shard_map(
        per_device, mesh=fine, in_specs=in_specs, out_specs=out_specs, check_vma=False
    )
```

```python
import math

import jax
import jax.numpy as jnp
from jax import lax
from jax.experimental import pallas as pl
from jax.experimental.pallas import tpu as pltpu
from jax.sharding import Mesh, PartitionSpec as P


DP = ("z", "xl", "y", "c")
SWAP = [(0, 1), (1, 0)]
UNROLL = 32
SMEM = pl.BlockSpec(memory_space=pltpu.SMEM)
VMEM = pl.BlockSpec(memory_space=pltpu.VMEM)


def dot_last(left, right, precision=None):
    return lax.dot_general(
        left, right, (((1,), (1,)), ((), ())), precision=precision, preferred_element_type=jnp.float32
    )


def dot_first(left, right):
    return lax.dot_general(
        left, right, (((0,), (0,)), ((), ())), preferred_element_type=jnp.float32
    )


def shift(value, axis, size, by):
    return lax.ppermute(value, axis, [(i, (i + by) % size) for i in range(size)])


def split3(value):
    high = value.astype(jnp.bfloat16)
    rest = value - high.astype(jnp.float32)
    middle = rest.astype(jnp.bfloat16)
    low = (rest - middle.astype(jnp.float32)).astype(jnp.bfloat16)
    return high, middle, low


def join3(parts):
    rows = parts.shape[0] // 4
    wide = parts.astype(jnp.float32)
    return wide[:rows] + wide[rows : 2 * rows] + wide[2 * rows : 3 * rows]


def store3(out, start, value):
    rows = value.shape[0]
    for i, part in enumerate(split3(value)):
        out[start + i * rows : start + (i + 1) * rows, :] = part
    out[start + 3 * rows : start + 4 * rows, :] = jnp.zeros((rows, value.shape[1]), jnp.bfloat16)


def local_call(body, out_shape, *args, scalars=0, **kwargs):
    return pl.pallas_call(
        body,
        out_shape=out_shape,
        in_specs=[SMEM] * scalars + [VMEM] * (len(args) - scalars),
        out_specs=jax.tree.map(lambda _: VMEM, out_shape),
        **kwargs,
    )(*args)


def pick_rows(rows, table, picked):
    def step(i, carry):
        for j in range(UNROLL):
            k = i * UNROLL + j
            picked[pl.ds(k, 1), :] = table[pl.ds(rows[k], 1), :]
        return carry

    lax.fori_loop(0, picked.shape[0] // UNROLL, step, 0)


def gather_kernel(rows, near, far, out, table, picked):
    half = near.shape[0]
    table[:half] = near[...].astype(jnp.float32)
    table[half:] = far[...].astype(jnp.float32)
    pick_rows(rows, table, picked)
    out[...] = picked[...].astype(out.dtype)


def gather(rows, near, far):
    count, lanes = rows.shape[0], near.shape[1]
    return pl.pallas_call(
        gather_kernel,
        out_shape=jax.ShapeDtypeStruct((count, lanes), near.dtype),
        in_specs=[SMEM, VMEM, VMEM],
        out_specs=VMEM,
        scratch_shapes=[
            pltpu.VMEM((2 * near.shape[0], lanes), jnp.float32),
            pltpu.VMEM((count, lanes), jnp.float32),
        ],
        compiler_params=pltpu.CompilerParams(vmem_limit_bytes=24 * 2**20),
        name="gather_rows",
    )(rows, near, far)


def forward_kernel(
    rows, near, far, upstream, v_proj, u_proj, groups, part, part16, bias_out, table, picked, staged, sems
):
    half = near.shape[0]
    rank = v_proj.shape[0]
    count, _, wide, lanes = groups.shape
    table[:half] = near[...].astype(jnp.float32)
    table[half:] = far[...].astype(jnp.float32)
    pick_rows(rows, table, picked)
    ones = jnp.ones((8, lanes), jnp.float32)
    h_sum = jnp.zeros((rank, lanes), jnp.float32)
    d_sum = jnp.zeros((rank, lanes), jnp.float32)
    copies = []
    for k in range(count):
        here = slice(k * wide, (k + 1) * wide)
        x = picked[here, :]
        scaled = upstream[here, :].astype(jnp.float32) * x
        x16 = x.astype(jnp.bfloat16)
        s16 = scaled.astype(jnp.bfloat16)
        staged[k, 0] = x16
        staged[k, 1] = s16
        copies.append(pltpu.make_async_copy(staged.at[k], groups.at[k], sems.at[k]))
        copies[-1].start()
        sums = dot_last(ones, scaled, lax.Precision.HIGHEST)
        for j in range(wide // 128):
            row = k * (wide // 128) + j
            bias_out[row : row + 1, :] = sums[:1, j * 128 : (j + 1) * 128]
        h_sum += jnp.dot(v_proj[:, here], x16, preferred_element_type=jnp.float32)
        d_sum += jnp.dot(u_proj[:, here], s16, preferred_element_type=jnp.float32)
    part[:rank] = h_sum
    part[rank:] = d_sum
    part16[:rank] = h_sum.astype(jnp.bfloat16)
    part16[rank:] = d_sum.astype(jnp.bfloat16)
    for copy in copies:
        copy.wait()


def forward(rows, near, far, upstream, v_proj, u_proj, count):
    half, lanes = near.shape
    rank = v_proj.shape[0]
    group = (count, 2, half // count, lanes)
    return pl.pallas_call(
        forward_kernel,
        out_shape=[
            jax.ShapeDtypeStruct(group, jnp.bfloat16),
            jax.ShapeDtypeStruct((2 * rank, lanes), jnp.float32),
            jax.ShapeDtypeStruct((2 * rank, lanes), jnp.bfloat16),
            jax.ShapeDtypeStruct((half // 128, 128), jnp.float32),
        ],
        in_specs=[SMEM] + [VMEM] * 5,
        out_specs=[pl.BlockSpec(memory_space=pltpu.HBM)] + [VMEM] * 3,
        scratch_shapes=[
            pltpu.VMEM((2 * half, lanes), jnp.float32),
            pltpu.VMEM((half, lanes), jnp.float32),
            pltpu.VMEM(group, jnp.bfloat16),
            pltpu.SemaphoreType.DMA((count,)),
        ],
        compiler_params=pltpu.CompilerParams(vmem_limit_bytes=40 * 2**20),
        name="gather_and_project",
    )(rows, near, far, upstream, v_proj, u_proj)


def ranks_kernel(part, other, bias, message):
    rows = part.shape[0]
    message[:rows] = (part[...] + other[...].astype(jnp.float32)).astype(jnp.bfloat16)
    store3(message, rows, bias[...])


def chip_kernel(*rest):
    *blocks, message = rest
    rows = (message.shape[0] - 128) // len(blocks)
    bias = jnp.zeros((32, 128), jnp.float32)
    for k, block in enumerate(blocks):
        message[k * rows : (k + 1) * rows, :] = block[:rows, :]
        bias += join3(block[rows:, :])
    store3(message, len(blocks) * rows, bias)


def grads_kernel(place, group, near_ranks, far_ranks, own, *rest):
    *pieces, result = rest
    count, _, wide, _ = group.shape
    ny = count // 2
    z_high, y, c = place[0], place[1], place[2]
    both = near_ranks.shape[0] // ny // 128 * 128
    rank = both // 2
    rows = rank // (len(pieces) + 1)
    for part in range(2):
        acc = jnp.zeros((rank, wide), jnp.float32)
        for k in range(ny):
            here = slice(k * both + part * rank, k * both + (part + 1) * rank)
            source = lax.rem(y + ny - k, ny) * 2
            left = jnp.concatenate([near_ranks[here, :], far_ranks[here, :]], axis=1)
            right = jnp.concatenate([group[source + c, 1 - part], group[source + 1 - c, 1 - part]], axis=1)
            acc = acc + dot_last(left, right)
        result[:, part * wide : (part + 1) * wide] = acc
    bias = join3(near_ranks[ny * both :, :]) + join3(far_ranks[ny * both :, :])
    own[:rows] = result[pl.ds(pl.multiple_of(z_high * rows, 32), rows), :]
    own[rows:] = jnp.zeros_like(own[rows:])
    own[rows:, :128] = bias[:16]
    own[rows:, 128:256] = bias[16:]
    parts = split3(bias)
    for k, piece in enumerate(pieces, 1):
        first = pl.multiple_of(lax.rem(z_high + k, len(pieces) + 1) * rows, 32)
        piece[:rows, :] = result[pl.ds(first, rows), :].astype(jnp.bfloat16)
        piece[rows:, :] = jnp.zeros((16, 2 * wide), jnp.bfloat16)
        for i, value in enumerate(parts):
            piece[rows:, i * 256 : i * 256 + 128] = value[:16]
            piece[rows:, i * 256 + 128 : i * 256 + 256] = value[16:]


def sum_kernel(place, own, first, second, third, keep, *rest):
    *messages, table = rest
    count, quarter, _ = table.shape
    rows = count * quarter
    total = own[:rows]
    bias = own[rows:, :256]
    for piece in (first, second, third):
        total += piece[:rows, :].astype(jnp.float32)
        for i in range(3):
            bias += piece[rows:, i * 256 : (i + 1) * 256].astype(jnp.float32)
    for q in range(count):
        table[q] = total[q * quarter : (q + 1) * quarter]
    low, xl = place[0], place[1]
    for out, flip_z, flip_x in zip((keep, *messages), (0, 1, 0, 1), (0, 0, 1, 1)):
        q = (1 - low if flip_z else low) * 2 + (1 - xl if flip_x else xl)
        out[:quarter] = table[q]
        out[quarter:] = jnp.zeros_like(out[quarter:])
        out[quarter:, :256] = bias


def split_kernel(place, keep, first, second, third, bias, *rest, norm):
    *shares, table = rest
    count, rows, _ = table.shape
    total = (keep[...] + first[...] + second[...] + third[...]) * norm
    bias[...] = total[count * rows :, :256]
    for k in range(count):
        table[k] = total[k * rows : (k + 1) * rows]
    for k, share in enumerate(shares):
        share[...] = table[lax.rem(place[0] + k, count)]


def pair_kernel(place, *rest):
    *shares, mine, theirs = rest
    count, rows, _ = mine.shape
    even = place[1] == 0
    for k, share in enumerate(shares):
        source = lax.rem(place[0] + count - k, count)
        low, high = share[:rows], share[rows:]
        mine[source] = jnp.where(even, low, high)
        theirs[source] = jnp.where(even, high, low)


def spread_kernel(place, mine, got, grad_u, grad_v):
    count, _, wide = mine.shape
    half = wide // 2
    even = place[1] == 0
    for k in range(count):
        for i in range(2):
            here = slice((2 * k + i) * half, (2 * k + i + 1) * half)
            value = jnp.where(even, mine[k], got[k]) if i == 0 else jnp.where(even, got[k], mine[k])
            grad_u[:, here] = value[:, :half]
            grad_v[:, here] = value[:, half:]


def inverse_rows(column_owner, first_column, count):
    wires = jnp.arange(column_owner.shape[0], dtype=jnp.int32)
    high = column_owner // 128 - first_column // 128
    low = column_owner % 128
    pick = (high[None, :] == jnp.arange(count // 128, dtype=jnp.int32)[:, None]).astype(jnp.bfloat16)
    lanes = low[:, None] == jnp.arange(128, dtype=jnp.int32)[None, :]
    values = jnp.concatenate(
        [
            jnp.where(lanes, (wires // 128)[:, None].astype(jnp.bfloat16), 0),
            jnp.where(lanes, (wires % 128)[:, None].astype(jnp.bfloat16), 0),
        ],
        axis=1,
    )
    found = jnp.dot(pick, values, preferred_element_type=jnp.float32).astype(jnp.int32)
    return (found[:, :128] * 128 + found[:, 128:]).reshape(-1)


def step(looked, column_owner, v_proj, u_proj, bias, upstream):
    z, xl, y, c, t = (lax.axis_index(a).astype(jnp.int32) for a in DP + ("t",))
    nz, ny = lax.axis_size("z"), lax.axis_size("y")
    dp_count = lax.axis_size(DP)
    block_rows = looked.shape[0]
    rank, half_width = v_proj.shape
    samples = upstream.shape[1]
    norm = 1.0 / math.sqrt(samples * dp_count)
    bf16 = jnp.bfloat16

    arrived = lax.all_to_all(looked, DP, split_axis=1, concat_axis=0, tiled=True)
    partner = lax.ppermute(arrived, "t", SWAP)
    wire = inverse_rows(column_owner, t * half_width, half_width)
    side = wire // block_rows % 2
    spot = wire // (2 * block_rows) * block_rows + wire % block_rows
    x_rows = jnp.where(side == t, 0, half_width) + spot
    groups, part, part16, bias_part = forward(
        x_rows, arrived, partner, upstream, v_proj, u_proj, 2 * ny
    )
    other = lax.ppermute(part16, "t", SWAP)
    group = lax.all_to_all(groups, ("y", "c"), split_axis=0, concat_axis=0, tiled=True)
    array = jax.ShapeDtypeStruct
    message = local_call(
        ranks_kernel, array((2 * rank + 128, samples), bf16), part, other, bias_part
    )
    hrank, dhrank = message[:rank], message[rank : 2 * rank]

    mix = dot_first(u_proj, hrank) + bias[:, None]
    cotan = upstream.astype(jnp.float32)
    dx_zero = (cotan * (mix + 1.0) + dot_first(v_proj, dhrank)).astype(bf16)
    dx_other = lax.ppermute(dx_zero, "t", SWAP)

    blocks = [message]
    for k in range(1, ny):
        blocks.append(shift(message, "y", ny, k))
    near_ranks = local_call(chip_kernel, array((2 * rank * ny + 128, samples), bf16), *blocks)
    far_ranks = lax.ppermute(near_ranks, "c", SWAP)
    wide = 2 * half_width // (2 * ny)
    rows = 2 * rank // nz
    own, *pieces = local_call(
        grads_kernel,
        [array((rows + 16, wide), jnp.float32)] + [array((rows + 16, wide), bf16)] * (nz // 2 - 1),
        jnp.stack([z // 2, y, c]),
        group,
        near_ranks,
        far_ranks,
        scalars=1,
        scratch_shapes=[pltpu.VMEM((rank, wide), jnp.float32)],
        compiler_params=pltpu.CompilerParams(vmem_limit_bytes=32 * 2**20),
    )
    pieces = [shift(p, "z", nz, 2 * k) for k, p in enumerate(pieces, 1)]

    columns = lax.dynamic_index_in_dim(
        column_owner.reshape(dp_count, 2, block_rows), t, 1, keepdims=False
    ).reshape(-1)
    out_rows = jnp.where(columns // half_width == t, 0, half_width) + columns % half_width
    outgoing = gather(out_rows, dx_zero, dx_other)
    d_looked = lax.all_to_all(outgoing, DP, split_axis=0, concat_axis=1, tiled=True)

    keep, *messages = local_call(
        sum_kernel,
        [array((rows // 4 + 16, wide), jnp.float32)] * 4,
        jnp.stack([z % 2, xl]),
        own,
        *pieces,
        scalars=1,
        scratch_shapes=[pltpu.VMEM((4, rows // 4, wide), jnp.float32)],
    )
    got = []
    for value, flip_z, flip_x in zip(messages, (1, 0, 1), (0, 1, 1)):
        pairs = [(i * 2 + j, (i ^ flip_z) * 2 + (j ^ flip_x)) for i in range(nz) for j in range(2)]
        got.append(lax.ppermute(value, ("z", "xl"), pairs))
    bias_sum, *shares = local_call(
        lambda *refs: split_kernel(*refs, norm=norm),
        [array((16, 256), jnp.float32)] + [array((rows // 4 // ny, wide), jnp.float32)] * ny,
        y[None],
        keep,
        *got,
        scalars=1,
        scratch_shapes=[pltpu.VMEM((ny, rows // 4 // ny, wide), jnp.float32)],
    )
    grad_bias = bias_sum.reshape(-1, 2, 128).transpose(1, 0, 2).reshape(-1)
    shares = [shares[0]] + [shift(shares[k], "y", ny, k) for k in range(1, ny)]
    place = jnp.stack([y, c])
    mine, theirs = local_call(
        pair_kernel,
        [array((ny, rows // 8 // ny, wide), jnp.float32)] * 2,
        place,
        *shares,
        scalars=1,
    )
    theirs = lax.ppermute(theirs, "c", SWAP)
    grad_u, grad_v = local_call(
        spread_kernel,
        [array((rows // 8 // ny, half_width), jnp.float32)] * 2,
        place,
        mine,
        theirs,
        scalars=1,
    )
    return (d_looked, grad_u, grad_v, grad_bias)


def solution(mesh):
    fine = Mesh(mesh.devices.reshape(8, 2, 4, 2, 2), DP + ("t",))
    in_specs = (
        P(DP + ("t",), None),
        P(),
        P(None, "t"),
        P(None, "t"),
        P("t"),
        P("t", DP),
    )
    out_specs = (P(DP + ("t",), None), P(DP, "t"), P(DP, "t"), P("t"))
    return jax.shard_map(step, mesh=fine, in_specs=in_specs, out_specs=out_specs, check_vma=False)
```

```python
import math

import jax
import jax.numpy as jnp
from jax import lax
from jax.experimental import pallas as pl
from jax.experimental.pallas import tpu as pltpu
from jax.sharding import Mesh, PartitionSpec as P


DP = ("z", "xl", "y", "c")
SWAP = [(0, 1), (1, 0)]
UNROLL = 32
CHUNK = 512


SMEM = pl.BlockSpec(memory_space=pltpu.SMEM)
VMEM = pl.BlockSpec(memory_space=pltpu.VMEM)


def dot_last(left, right, precision=None):
    return lax.dot_general(
        left, right, (((1,), (1,)), ((), ())), precision=precision, preferred_element_type=jnp.float32
    )


def dot_first(left, right):
    return lax.dot_general(
        left, right, (((0,), (0,)), ((), ())), preferred_element_type=jnp.float32
    )


def shift(value, axis, size, by):
    return lax.ppermute(value, axis, [(i, (i + by) % size) for i in range(size)])


def split3(value):
    high = value.astype(jnp.bfloat16)
    rest = value - high.astype(jnp.float32)
    middle = rest.astype(jnp.bfloat16)
    low = (rest - middle.astype(jnp.float32)).astype(jnp.bfloat16)
    return high, middle, low


def join3(parts):
    rows = parts.shape[0] // 4
    wide = parts.astype(jnp.float32)
    return wide[:rows] + wide[rows : 2 * rows] + wide[2 * rows : 3 * rows]


def store3(out, start, value):
    rows = value.shape[0]
    for i, part in enumerate(split3(value)):
        out[start + i * rows : start + (i + 1) * rows, :] = part
    out[start + 3 * rows : start + 4 * rows, :] = jnp.zeros((rows, value.shape[1]), jnp.bfloat16)


def local_call(body, out_shape, *args, scalars=0, mib, specs=None, **kwargs):
    return pl.pallas_call(
        body,
        out_shape=out_shape,
        in_specs=specs or [SMEM] * scalars + [VMEM] * (len(args) - scalars),
        out_specs=jax.tree.map(lambda _: VMEM, out_shape),
        compiler_params=pltpu.CompilerParams(vmem_limit_bytes=mib * 2**20),
        **kwargs,
    )(*args)


def pick_rows(rows, table, picked):
    def step(i, carry):
        for j in range(UNROLL):
            k = i * UNROLL + j
            picked[pl.ds(k, 1), :] = table[pl.ds(rows[k], 1), :]
        return carry

    lax.fori_loop(0, picked.shape[0] // UNROLL, step, 0)


def gather_kernel(rows, near, far, extra, out, table, picked):
    half = near.shape[0]
    dests, height, lanes = out.shape
    block = height - extra.shape[1]
    table[:half] = near[...].astype(jnp.float32)
    table[half:] = far[...].astype(jnp.float32)
    pick_rows(rows, table, picked)
    out[:, :block, :] = picked[...].reshape(dests, block, lanes).astype(out.dtype)
    out[:, block:, :] = extra[...]


def gather(rows, near, far, extra):
    count, lanes = rows.shape[0], near.shape[1]
    dests, height, _ = extra.shape
    return pl.pallas_call(
        gather_kernel,
        out_shape=jax.ShapeDtypeStruct((dests, count // dests + height, lanes), near.dtype),
        in_specs=[SMEM, VMEM, VMEM, VMEM],
        out_specs=VMEM,
        scratch_shapes=[
            pltpu.VMEM((2 * near.shape[0], lanes), jnp.float32),
            pltpu.VMEM((count, lanes), jnp.float32),
        ],
        compiler_params=pltpu.CompilerParams(vmem_limit_bytes=16 * 2**20),
        name="gather_rows",
    )(rows, near, far, extra)


def forward_kernel(rows, near, far, *rest):
    sources, (x_out, part, part16, bias_out, table, picked, *copied, sems) = rest[:3], rest[3:]
    copies = [pltpu.make_async_copy(a, b, sems.at[i]) for i, (a, b) in enumerate(zip(sources, copied))]
    for copy in copies:
        copy.start()
    upstream, v_proj, u_proj = copied
    half, lanes = near.shape
    rank = v_proj.shape[0]
    table[:half] = near[...].astype(jnp.float32)
    table[half:] = far[...].astype(jnp.float32)
    pick_rows(rows, table, picked)
    for copy in copies:
        copy.wait()
    ones = jnp.ones((8, lanes), jnp.float32)
    h_sum = jnp.zeros((rank, lanes), jnp.float32)
    d_sum = jnp.zeros((rank, lanes), jnp.float32)
    for k in range(half // CHUNK):
        here = slice(k * CHUNK, (k + 1) * CHUNK)
        x = picked[here, :]
        scaled = upstream[here, :].astype(jnp.float32) * x
        x16 = x.astype(jnp.bfloat16)
        x_out[here, :] = x16
        sums = dot_last(ones, scaled, lax.Precision.HIGHEST)
        for j in range(CHUNK // 128):
            row = k * (CHUNK // 128) + j
            bias_out[row : row + 1, :] = sums[:1, j * 128 : (j + 1) * 128]
        h_sum += jnp.dot(v_proj[:, here], x16, preferred_element_type=jnp.float32)
        d_sum += jnp.dot(
            u_proj[:, here], scaled.astype(jnp.bfloat16), preferred_element_type=jnp.float32
        )
    part[:rank] = h_sum
    part[rank:] = d_sum
    part16[:rank] = h_sum.astype(jnp.bfloat16)
    part16[rank:] = d_sum.astype(jnp.bfloat16)


def ranks_kernel(part, other, bias, ranks, message, total):
    rows = part.shape[0]
    value = part[...] + other[...].astype(jnp.float32)
    ranks[...] = value.astype(jnp.bfloat16)
    total[...] = value
    step = rows // 2 // 128
    for i in range(2):
        for j in range(step):
            to = i * rows // 2 + j * 128
            rank_rows = total[pl.ds(i * rows // 2 + j, 128, stride=step), :]
            message[to : to + 128, :] = rank_rows.astype(jnp.bfloat16)
    store3(message, rows, bias[...])


def join_kernel(*rest):
    *blocks, message = rest
    rows = (message.shape[0] - 128) // len(blocks)
    bias = jnp.zeros((32, 128), jnp.float32)
    for k, block in enumerate(blocks):
        message[k * rows : (k + 1) * rows, :] = block[:rows, :]
        bias += join3(block[rows:, :])
    store3(message, len(blocks) * rows, bias)


def join_blocks(blocks):
    rows, lanes = blocks[0].shape
    shape = jax.ShapeDtypeStruct(((rows - 128) * len(blocks) + 128, lanes), blocks[0].dtype)
    return local_call(join_kernel, shape, *blocks, mib=6)


def grads_kernel(place, x_group, up_group, near_ranks, far_ranks, pieces, result, spread, bias_rows):
    count, wide, lanes = x_group.shape
    ny = count // 2
    y, c = place[0], place[1]
    both = near_ranks.shape[0] // ny // 128 * 128
    rank = both // 2
    for part in range(2):
        acc = jnp.zeros((rank, wide), jnp.float32)
        for k in range(ny):
            here = slice(k * both + part * rank, k * both + (part + 1) * rank)
            pair = lax.rem(y + ny - k, ny) * 2
            left = jnp.concatenate([near_ranks[here, :], far_ranks[here, :]], axis=1)
            right = [x_group[pair + c], x_group[pair + 1 - c]]
            if part == 0:
                ups = [up_group[pair + c], up_group[pair + 1 - c]]
                right = [
                    (up.astype(jnp.float32) * x.astype(jnp.float32)).astype(jnp.bfloat16)
                    for up, x in zip(ups, right)
                ]
            acc = acc + dot_last(left, jnp.concatenate(right, axis=1))
        result[:, part * wide : (part + 1) * wide] = acc
    dests, height, _ = pieces.shape
    blocks = 2 * wide // lanes
    for j in range(rank // dests):
        for k in range(blocks):
            spread[pl.ds(j * blocks + k, dests, stride=height), :] = result[
                j * dests : (j + 1) * dests, k * lanes : (k + 1) * lanes
            ]
    bias = join3(near_ranks[ny * both :, :]) + join3(far_ranks[ny * both :, :])
    bias_rows[...] = bias
    mine = (y * 2 + c) * (wide // lanes)
    first = rank // dests * blocks
    for k in range(wide // lanes):
        row = bias_rows[pl.ds(mine + k, 1), :]
        high = row.astype(jnp.bfloat16).astype(jnp.float32)
        for i, value in enumerate((high, row - high)):
            at = first + i * (wide // lanes) + k
            spread[pl.ds(at, dests, stride=height), :] = jnp.broadcast_to(value, (dests, lanes))
    pieces[...] = spread[...].reshape(dests, height, lanes).astype(jnp.bfloat16)


def arrive_kernel(got, d_looked, grad_u, grad_v, grad_bias, *, block, wide, norm):
    sources, height, lanes = got.shape
    for k in range(sources):
        d_looked[:, k * lanes : (k + 1) * lanes] = got[k, :block, :]
    columns = wide // lanes
    group = grad_u.shape[1] // wide
    first = 2 * columns * grad_u.shape[0]
    for b in range(group):
        total = jnp.zeros((height - block, lanes), jnp.float32)
        for k in range(sources // group):
            total += got[k * group + b, block:, :].astype(jnp.float32)
        total = total * norm
        for k in range(columns):
            here = slice(b * wide + k * lanes, b * wide + (k + 1) * lanes)
            for j in range(grad_u.shape[0]):
                row = j * 2 * columns + k
                grad_u[j : j + 1, here] = total[row : row + 1]
                grad_v[j : j + 1, here] = total[row + columns : row + columns + 1]
            row = first + k
            grad_bias[b * columns + k : b * columns + k + 1, :] = (
                total[row : row + 1] + total[row + columns : row + columns + 1]
            )


def inverse_rows(column_owner, first_column, count):
    wires = jnp.arange(column_owner.shape[0], dtype=jnp.int32)
    high = column_owner // 128 - first_column // 128
    low = column_owner % 128
    pick = (high[None, :] == jnp.arange(count // 128, dtype=jnp.int32)[:, None]).astype(jnp.bfloat16)
    lanes = low[:, None] == jnp.arange(128, dtype=jnp.int32)[None, :]
    values = jnp.concatenate(
        [
            jnp.where(lanes, (wires // 128)[:, None].astype(jnp.bfloat16), 0),
            jnp.where(lanes, (wires % 128)[:, None].astype(jnp.bfloat16), 0),
        ],
        axis=1,
    )
    found = jnp.dot(pick, values, preferred_element_type=jnp.float32).astype(jnp.int32)
    return (found[:, :128] * 128 + found[:, 128:]).reshape(-1)


def step(looked, column_owner, v_proj, u_proj, bias, upstream):
    y, c, t = (lax.axis_index(a).astype(jnp.int32) for a in ("y", "c", "t"))
    ny = lax.axis_size("y")
    dp_count = lax.axis_size(DP)
    block_rows = looked.shape[0]
    rank, half_width = v_proj.shape
    samples = upstream.shape[1]
    norm = 1.0 / math.sqrt(samples * dp_count)
    bf16 = jnp.bfloat16

    array = jax.ShapeDtypeStruct
    group = 2 * ny
    wide = half_width // group
    arrived = lax.all_to_all(looked, DP, split_axis=1, concat_axis=0, tiled=True)
    partner = lax.ppermute(arrived, "t", SWAP)
    up_group = lax.all_to_all(
        upstream.reshape(group, wide, samples), ("y", "c"), split_axis=0, concat_axis=0, tiled=True
    )
    wire = inverse_rows(column_owner, t * half_width, half_width)
    side = wire // block_rows % 2
    spot = wire // (2 * block_rows) * block_rows + wire % block_rows
    x_rows = jnp.where(side == t, 0, half_width) + spot
    hbm = pltpu.with_memory_space_constraint
    x_zero, part, part16, bias_part = local_call(
        forward_kernel,
        [
            array((half_width, samples), bf16),
            array((2 * rank, samples), jnp.float32),
            array((2 * rank, samples), bf16),
            array((half_width // 128, 128), jnp.float32),
        ],
        x_rows,
        arrived,
        partner,
        upstream,
        hbm(v_proj, pltpu.HBM),
        hbm(u_proj, pltpu.HBM),
        scalars=1,
        scratch_shapes=[
            pltpu.VMEM((2 * half_width, samples), jnp.float32),
            pltpu.VMEM((half_width, samples), jnp.float32),
            pltpu.VMEM(upstream.shape, bf16),
            pltpu.VMEM(v_proj.shape, bf16),
            pltpu.VMEM(u_proj.shape, bf16),
            pltpu.SemaphoreType.DMA((3,)),
        ],
        specs=[SMEM, VMEM, VMEM] + [pl.BlockSpec(memory_space=pltpu.HBM)] * 3,
        mib=28,
    )
    other = lax.ppermute(part16, "t", SWAP)
    x_group = lax.all_to_all(
        x_zero.reshape(group, wide, samples), ("y", "c"), split_axis=0, concat_axis=0, tiled=True
    )
    ranks, message = local_call(
        ranks_kernel,
        [array((2 * rank, samples), bf16), array((2 * rank + 128, samples), bf16)],
        part,
        other,
        bias_part,
        scratch_shapes=[pltpu.VMEM((2 * rank, samples), jnp.float32)],
        mib=4,
    )

    mix = dot_first(u_proj, ranks[:rank]) + bias[:, None]
    cotan = upstream.astype(jnp.float32)
    dx_zero = (cotan * (mix + 1.0) + dot_first(v_proj, ranks[rank:])).astype(bf16)
    dx_other = lax.ppermute(dx_zero, "t", SWAP)

    blocks = [message]
    for k in range(1, ny):
        blocks.append(shift(blocks[0], "y", ny, k))
    near_ranks = join_blocks(blocks)
    far_ranks = lax.ppermute(near_ranks, "c", SWAP)
    height = rank // dp_count * (2 * wide // 128) + 2 * wide // 128
    pieces = local_call(
        grads_kernel,
        array((dp_count, height, 128), bf16),
        jnp.stack([y, c]),
        x_group,
        up_group,
        near_ranks,
        far_ranks,
        scalars=1,
        scratch_shapes=[
            pltpu.VMEM((rank, 2 * wide), jnp.float32),
            pltpu.VMEM((dp_count * height, 128), jnp.float32),
            pltpu.VMEM((32, 128), jnp.float32),
        ],
        mib=16,
    )

    columns = lax.dynamic_index_in_dim(
        column_owner.reshape(dp_count, 2, block_rows), t, 1, keepdims=False
    ).reshape(-1)
    out_rows = jnp.where(columns // half_width == t, 0, half_width) + columns % half_width
    outgoing = gather(out_rows, dx_zero, dx_other, pieces)
    got = lax.all_to_all(outgoing, DP, split_axis=0, concat_axis=0, tiled=True)
    d_looked, grad_u, grad_v, grad_bias = local_call(
        lambda *refs: arrive_kernel(*refs, block=block_rows, wide=wide, norm=norm),
        [
            array((block_rows, dp_count * samples), bf16),
            array((rank // dp_count, half_width), jnp.float32),
            array((rank // dp_count, half_width), jnp.float32),
            array((half_width // 128, 128), jnp.float32),
        ],
        got,
        mib=8,
    )
    return (d_looked, grad_u, grad_v, grad_bias.reshape(-1))


def solution(mesh):
    fine = Mesh(mesh.devices.reshape(8, 2, 4, 2, 2), DP + ("t",))
    in_specs = (
        P(DP + ("t",), None),
        P(),
        P(None, "t"),
        P(None, "t"),
        P("t"),
        P("t", DP),
    )
    out_specs = (P(DP + ("t",), None), P(DP, "t"), P(DP, "t"), P("t"))
    return jax.shard_map(step, mesh=fine, in_specs=in_specs, out_specs=out_specs, check_vma=False)
```

```python
import math

import jax
import jax.numpy as jnp
from jax import lax
from jax.experimental import pallas as pl
from jax.experimental.pallas import tpu as pltpu
from jax.sharding import Mesh, PartitionSpec as P


DP = ("z", "xl", "y", "c")
SWAP = [(0, 1), (1, 0)]
UNROLL = 32
CHUNK = 512


SMEM = pl.BlockSpec(memory_space=pltpu.SMEM)
VMEM = pl.BlockSpec(memory_space=pltpu.VMEM)


def dot_last(left, right):
    return lax.dot_general(
        left, right, (((1,), (1,)), ((), ())), preferred_element_type=jnp.float32
    )


def shift(value, axis, size, by):
    return lax.ppermute(value, axis, [(i, (i + by) % size) for i in range(size)])


def split3(value):
    high = value.astype(jnp.bfloat16)
    rest = value - high.astype(jnp.float32)
    middle = rest.astype(jnp.bfloat16)
    low = (rest - middle.astype(jnp.float32)).astype(jnp.bfloat16)
    return high, middle, low


def join3(parts):
    rows = parts.shape[0] // 4
    wide = parts.astype(jnp.float32)
    return wide[:rows] + wide[rows : 2 * rows] + wide[2 * rows : 3 * rows]


def store3(out, start, value):
    rows = value.shape[0]
    for i, part in enumerate(split3(value)):
        out[start + i * rows : start + (i + 1) * rows, :] = part
    out[start + 3 * rows : start + 4 * rows, :] = jnp.zeros((rows, value.shape[1]), jnp.bfloat16)


def local_call(body, out_shape, *args, scalars=0, mib, specs=None, **kwargs):
    return pl.pallas_call(
        body,
        out_shape=out_shape,
        in_specs=specs or [SMEM] * scalars + [VMEM] * (len(args) - scalars),
        out_specs=jax.tree.map(lambda _: VMEM, out_shape),
        compiler_params=pltpu.CompilerParams(vmem_limit_bytes=mib * 2**20),
        **kwargs,
    )(*args)


def pick_rows(rows, table, picked):
    def step(i, carry):
        for j in range(UNROLL):
            k = i * UNROLL + j
            picked[pl.ds(k, 1), :] = table[pl.ds(rows[k], 1), :]
        return carry

    lax.fori_loop(0, picked.shape[0] // UNROLL, step, 0)


def gather_kernel(rows, near, far, extra, out, table, picked):
    half = near.shape[0]
    dests, height, lanes = out.shape
    block = height - extra.shape[1]
    table[:half] = near[...].astype(jnp.float32)
    table[half:] = far[...].astype(jnp.float32)
    pick_rows(rows, table, picked)
    out[:, :block, :] = picked[...].reshape(dests, block, lanes).astype(out.dtype)
    out[:, block:, :] = extra[...]


def gather(rows, near, far, extra):
    count, lanes = rows.shape[0], near.shape[1]
    dests, height, _ = extra.shape
    return pl.pallas_call(
        gather_kernel,
        out_shape=jax.ShapeDtypeStruct((dests, count // dests + height, lanes), near.dtype),
        in_specs=[SMEM, VMEM, VMEM, VMEM],
        out_specs=VMEM,
        scratch_shapes=[
            pltpu.VMEM((2 * near.shape[0], lanes), jnp.float32),
            pltpu.VMEM((count, lanes), jnp.float32),
        ],
        compiler_params=pltpu.CompilerParams(vmem_limit_bytes=16 * 2**20),
        name="gather_rows",
    )(rows, near, far, extra)


def forward_kernel(rows, near, far, *rest):
    sources, (x_out, part, part16, table, picked, *copied, sems) = rest[:3], rest[3:]
    copies = [pltpu.make_async_copy(a, b, sems.at[i]) for i, (a, b) in enumerate(zip(sources, copied))]
    for copy in copies:
        copy.start()
    upstream, v_proj, u_proj = copied
    half, lanes = near.shape
    rank = v_proj.shape[0]
    table[:half] = near[...].astype(jnp.float32)
    table[half:] = far[...].astype(jnp.float32)
    pick_rows(rows, table, picked)
    for copy in copies:
        copy.wait()
    ones = jnp.ones((8, 3 * lanes), jnp.bfloat16)
    h_sum = jnp.zeros((rank, lanes), jnp.float32)
    d_sum = jnp.zeros((rank, lanes), jnp.float32)
    for k in range(half // CHUNK):
        here = slice(k * CHUNK, (k + 1) * CHUNK)
        x = picked[here, :]
        scaled = upstream[here, :].astype(jnp.float32) * x
        x16 = x.astype(jnp.bfloat16)
        x_out[here, :] = x16
        sums = dot_last(ones, jnp.concatenate(split3(scaled), axis=1))
        for j in range(CHUNK // 128):
            row = k * (CHUNK // 128) + j
            part[2 * rank + row : 2 * rank + row + 1, :] = sums[:1, j * 128 : (j + 1) * 128]
        h_sum += jnp.dot(v_proj[:, here], x16, preferred_element_type=jnp.float32)
        d_sum += jnp.dot(
            u_proj[:, here], scaled.astype(jnp.bfloat16), preferred_element_type=jnp.float32
        )
    part[:rank] = h_sum
    part[rank : 2 * rank] = d_sum
    part16[:rank] = h_sum.astype(jnp.bfloat16)
    part16[rank:] = d_sum.astype(jnp.bfloat16)


def ranks_kernel(part, other, bias, upstream_in, v_in, u_in, message, dx, upstream, v_proj, u_proj, total, sems):
    rows = other.shape[0]
    rank = rows // 2
    count = upstream.shape[0] // CHUNK
    copies = []
    for k in range(count):
        here = slice(k * CHUNK, (k + 1) * CHUNK)
        pairs = (
            (u_in.at[:, here], u_proj.at[:, here]),
            (v_in.at[:, here], v_proj.at[:, here]),
            (upstream_in.at[here], upstream.at[here]),
        )
        copies.append([pltpu.make_async_copy(a, b, sems.at[k, i]) for i, (a, b) in enumerate(pairs)])
        for copy in copies[-1]:
            copy.start()
    value = part[:rows] + other[...].astype(jnp.float32)
    total[...] = value
    step = rank // 128
    for i in range(2):
        for j in range(step):
            to = i * rank + j * 128
            rank_rows = total[pl.ds(i * rank + j, 128, stride=step), :]
            message[to : to + 128, :] = rank_rows.astype(jnp.bfloat16)
    store3(message, rows, part[rows:])
    h_turned = value[:rank].T.astype(jnp.bfloat16)
    d_turned = value[rank:].T.astype(jnp.bfloat16)
    for k in range(count):
        here = slice(k * CHUNK, (k + 1) * CHUNK)
        for copy in copies[k]:
            copy.wait()
        mix = jnp.dot(h_turned, u_proj[:, here], preferred_element_type=jnp.float32)
        mix = (mix + bias[k : k + 1, :]).T
        back = jnp.dot(d_turned, v_proj[:, here], preferred_element_type=jnp.float32).T
        dx[here, :] = (upstream[here, :].astype(jnp.float32) * (mix + 1.0) + back).astype(jnp.bfloat16)


def grads_kernel(place, x_group, up_group, *rest):
    *ranks, pieces, result, spread, bias_rows = rest
    count, wide, lanes = x_group.shape
    ny = count // 2
    y, c = place[0], place[1]
    rank = (ranks[0].shape[0] - 128) // 2
    for part in range(2):
        here = slice(part * rank, (part + 1) * rank)
        acc = jnp.zeros((rank, wide), jnp.float32)
        for k in range(ny):
            pair = lax.rem(y + ny - k, ny) * 2
            left = jnp.concatenate([ranks[k][here, :], ranks[ny + k][here, :]], axis=1)
            right = [x_group[pair + c], x_group[pair + 1 - c]]
            if part == 0:
                ups = [up_group[pair + c], up_group[pair + 1 - c]]
                right = [
                    (up.astype(jnp.float32) * x.astype(jnp.float32)).astype(jnp.bfloat16)
                    for up, x in zip(ups, right)
                ]
            acc = acc + dot_last(left, jnp.concatenate(right, axis=1))
        result[:, part * wide : (part + 1) * wide] = acc
    dests, height, _ = pieces.shape
    blocks = 2 * wide // lanes
    for j in range(rank // dests):
        for k in range(blocks):
            spread[pl.ds(j * blocks + k, dests, stride=height), :] = result[
                j * dests : (j + 1) * dests, k * lanes : (k + 1) * lanes
            ]
    bias_rows[...] = sum(join3(block[2 * rank :, :]) for block in ranks)
    mine = (y * 2 + c) * (wide // lanes)
    first = rank // dests * blocks
    for k in range(wide // lanes):
        row = bias_rows[pl.ds(mine + k, 1), :]
        high = row.astype(jnp.bfloat16).astype(jnp.float32)
        for i, value in enumerate((high, row - high)):
            at = first + i * (wide // lanes) + k
            spread[pl.ds(at, dests, stride=height), :] = jnp.broadcast_to(value, (dests, lanes))
    pieces[...] = spread[...].reshape(dests, height, lanes).astype(jnp.bfloat16)


def arrive_kernel(got, d_looked, grad_u, grad_v, grad_bias, *, block, wide, norm):
    sources, height, lanes = got.shape
    for k in range(sources):
        d_looked[:, k * lanes : (k + 1) * lanes] = got[k, :block, :]
    columns = wide // lanes
    group = grad_u.shape[1] // wide
    first = 2 * columns * grad_u.shape[0]
    for b in range(group):
        total = jnp.zeros((height - block, lanes), jnp.float32)
        for k in range(sources // group):
            total += got[k * group + b, block:, :].astype(jnp.float32)
        total = total * norm
        for k in range(columns):
            here = slice(b * wide + k * lanes, b * wide + (k + 1) * lanes)
            for j in range(grad_u.shape[0]):
                row = j * 2 * columns + k
                grad_u[j : j + 1, here] = total[row : row + 1]
                grad_v[j : j + 1, here] = total[row + columns : row + columns + 1]
            row = first + k
            grad_bias[b * columns + k : b * columns + k + 1, :] = (
                total[row : row + 1] + total[row + columns : row + columns + 1]
            )


def inverse_rows(column_owner, first_column, count):
    wires = jnp.arange(column_owner.shape[0], dtype=jnp.int32)
    high = column_owner // 128 - first_column // 128
    low = column_owner % 128
    pick = (high[None, :] == jnp.arange(count // 128, dtype=jnp.int32)[:, None]).astype(jnp.bfloat16)
    lanes = low[:, None] == jnp.arange(128, dtype=jnp.int32)[None, :]
    values = jnp.concatenate(
        [
            jnp.where(lanes, (wires // 128)[:, None].astype(jnp.bfloat16), 0),
            jnp.where(lanes, (wires % 128)[:, None].astype(jnp.bfloat16), 0),
        ],
        axis=1,
    )
    found = jnp.dot(pick, values, preferred_element_type=jnp.float32).astype(jnp.int32)
    return (found[:, :128] * 128 + found[:, 128:]).reshape(-1)


def step(looked, column_owner, v_proj, u_proj, bias, upstream):
    y, c, t = (lax.axis_index(a).astype(jnp.int32) for a in ("y", "c", "t"))
    ny = lax.axis_size("y")
    dp_count = lax.axis_size(DP)
    block_rows = looked.shape[0]
    rank, half_width = v_proj.shape
    samples = upstream.shape[1]
    norm = 1.0 / math.sqrt(samples * dp_count)
    bf16 = jnp.bfloat16

    array = jax.ShapeDtypeStruct
    group = 2 * ny
    wide = half_width // group
    arrived = lax.all_to_all(looked, DP, split_axis=1, concat_axis=0, tiled=True)
    partner = lax.ppermute(arrived, "t", SWAP)
    up_group = lax.all_to_all(
        upstream.reshape(group, wide, samples), ("y", "c"), split_axis=0, concat_axis=0, tiled=True
    )
    wire = inverse_rows(column_owner, t * half_width, half_width)
    side = wire // block_rows % 2
    spot = wire // (2 * block_rows) * block_rows + wire % block_rows
    x_rows = jnp.where(side == t, 0, half_width) + spot
    hbm = pltpu.with_memory_space_constraint
    x_zero, part, part16 = local_call(
        forward_kernel,
        [
            array((half_width, samples), bf16),
            array((2 * rank + half_width // 128, samples), jnp.float32),
            array((2 * rank, samples), bf16),
        ],
        x_rows,
        arrived,
        partner,
        hbm(upstream, pltpu.HBM),
        hbm(v_proj, pltpu.HBM),
        hbm(u_proj, pltpu.HBM),
        scalars=1,
        scratch_shapes=[
            pltpu.VMEM((2 * half_width, samples), jnp.float32),
            pltpu.VMEM((half_width, samples), jnp.float32),
            pltpu.VMEM(upstream.shape, bf16),
            pltpu.VMEM(v_proj.shape, bf16),
            pltpu.VMEM(u_proj.shape, bf16),
            pltpu.SemaphoreType.DMA((3,)),
        ],
        specs=[SMEM, VMEM, VMEM] + [pl.BlockSpec(memory_space=pltpu.HBM)] * 3,
        mib=28,
    )
    other = lax.ppermute(part16, "t", SWAP)
    x_group = lax.all_to_all(
        x_zero.reshape(group, wide, samples), ("y", "c"), split_axis=0, concat_axis=0, tiled=True
    )
    message, dx_zero = local_call(
        ranks_kernel,
        [array((2 * rank + 128, samples), bf16), array((half_width, samples), bf16)],
        part,
        other,
        bias.reshape(-1, CHUNK),
        hbm(upstream, pltpu.HBM),
        hbm(v_proj, pltpu.HBM),
        hbm(u_proj, pltpu.HBM),
        scratch_shapes=[
            pltpu.VMEM(upstream.shape, bf16),
            pltpu.VMEM(v_proj.shape, bf16),
            pltpu.VMEM(u_proj.shape, bf16),
            pltpu.VMEM((2 * rank, samples), jnp.float32),
            pltpu.SemaphoreType.DMA((half_width // CHUNK, 3)),
        ],
        specs=[VMEM] * 3 + [pl.BlockSpec(memory_space=pltpu.HBM)] * 3,
        mib=20,
    )
    dx_other = lax.ppermute(dx_zero, "t", SWAP)

    blocks = [message]
    for k in range(1, ny):
        blocks.append(shift(message, "y", ny, k))
    blocks = blocks + [lax.ppermute(block, "c", SWAP) for block in blocks]
    height = rank // dp_count * (2 * wide // 128) + 2 * wide // 128
    pieces = local_call(
        grads_kernel,
        array((dp_count, height, 128), bf16),
        jnp.stack([y, c]),
        x_group,
        up_group,
        *blocks,
        scalars=1,
        scratch_shapes=[
            pltpu.VMEM((rank, 2 * wide), jnp.float32),
            pltpu.VMEM((dp_count * height, 128), jnp.float32),
            pltpu.VMEM((32, 128), jnp.float32),
        ],
        mib=16,
    )

    columns = lax.dynamic_index_in_dim(
        column_owner.reshape(dp_count, 2, block_rows), t, 1, keepdims=False
    ).reshape(-1)
    out_rows = jnp.where(columns // half_width == t, 0, half_width) + columns % half_width
    outgoing = gather(out_rows, dx_zero, dx_other, pieces)
    got = lax.all_to_all(outgoing, DP, split_axis=0, concat_axis=0, tiled=True)
    d_looked, grad_u, grad_v, grad_bias = local_call(
        lambda *refs: arrive_kernel(*refs, block=block_rows, wide=wide, norm=norm),
        [
            array((block_rows, dp_count * samples), bf16),
            array((rank // dp_count, half_width), jnp.float32),
            array((rank // dp_count, half_width), jnp.float32),
            array((half_width // 128, 128), jnp.float32),
        ],
        got,
        mib=8,
    )
    return (d_looked, grad_u, grad_v, grad_bias.reshape(-1))


def solution(mesh):
    fine = Mesh(mesh.devices.reshape(8, 2, 4, 2, 2), DP + ("t",))
    in_specs = (
        P(DP + ("t",), None),
        P(),
        P(None, "t"),
        P(None, "t"),
        P("t"),
        P("t", DP),
    )
    out_specs = (P(DP + ("t",), None), P(DP, "t"), P(DP, "t"), P("t"))
    return jax.shard_map(step, mesh=fine, in_specs=in_specs, out_specs=out_specs, check_vma=False)
```

```python
import math

import jax
import jax.numpy as jnp
from jax import lax
from jax.experimental import pallas as pl
from jax.experimental.pallas import tpu as pltpu
from jax.sharding import Mesh, PartitionSpec as P


DP = ("z", "xl", "y", "c")
SWAP = [(0, 1), (1, 0)]
UNROLL = 32
CHUNK = 512


SMEM = pl.BlockSpec(memory_space=pltpu.SMEM)
VMEM = pl.BlockSpec(memory_space=pltpu.VMEM)
HBM = pl.BlockSpec(memory_space=pltpu.HBM)


def dot_last(left, right):
    return lax.dot_general(
        left, right, (((1,), (1,)), ((), ())), preferred_element_type=jnp.float32
    )


def dot_first(left, right):
    return lax.dot_general(
        left, right, (((0,), (0,)), ((), ())), preferred_element_type=jnp.float32
    )


def shift(value, axis, size, by):
    return lax.ppermute(value, axis, [(i, (i + by) % size) for i in range(size)])


def split3(value):
    high = value.astype(jnp.bfloat16)
    rest = value - high.astype(jnp.float32)
    middle = rest.astype(jnp.bfloat16)
    low = (rest - middle.astype(jnp.float32)).astype(jnp.bfloat16)
    return high, middle, low


def join3(parts):
    rows = parts.shape[0] // 4
    wide = parts.astype(jnp.float32)
    return wide[:rows] + wide[rows : 2 * rows] + wide[2 * rows : 3 * rows]


def store3(out, start, value):
    rows = value.shape[0]
    for i, part in enumerate(split3(value)):
        out[start + i * rows : start + (i + 1) * rows, :] = part
    out[start + 3 * rows : start + 4 * rows, :] = jnp.zeros((rows, value.shape[1]), jnp.bfloat16)


def local_call(body, out_shape, *args, scalars=0, mib, specs=None, **kwargs):
    return pl.pallas_call(
        body,
        out_shape=out_shape,
        in_specs=specs or [SMEM] * scalars + [VMEM] * (len(args) - scalars),
        out_specs=jax.tree.map(lambda _: VMEM, out_shape),
        compiler_params=pltpu.CompilerParams(vmem_limit_bytes=mib * 2**20),
        **kwargs,
    )(*args)


def pick_rows(rows, table, picked):
    def step(i, carry):
        for j in range(UNROLL):
            k = i * UNROLL + j
            picked[pl.ds(k, 1), :] = table[pl.ds(rows[k], 1), :]
        return carry

    lax.fori_loop(0, picked.shape[0] // UNROLL, step, 0)


def start_copies(pairs, sems):
    copies = [pltpu.make_async_copy(a, b, sems.at[i]) for i, (a, b) in enumerate(pairs)]
    for copy in copies:
        copy.start()
    return copies


def in_hbm(*values):
    return [pltpu.with_memory_space_constraint(value, pltpu.HBM) for value in values]


def gather_kernel(rows_in, near_in, far_in, extra, out, rows, near, far, table, picked, sems):
    half = near.shape[0]
    dests, height, lanes = out.shape
    block = height - extra.shape[1]
    pairs = ((near_in, near), (far_in, far), (rows_in, rows), (extra, out.at[:, block:, :]))
    copies = start_copies(pairs, sems)
    copies[0].wait()
    table[:half] = near[...].astype(jnp.float32)
    copies[1].wait()
    table[half:] = far[...].astype(jnp.float32)
    copies[2].wait()
    pick_rows(rows, table, picked)
    out[:, :block, :] = picked[...].reshape(dests, block, lanes).astype(out.dtype)
    copies[3].wait()


def gather(rows, near, far, extra):
    count, lanes = rows.shape[0], near.shape[1]
    dests, height, _ = extra.shape
    return pl.pallas_call(
        gather_kernel,
        out_shape=jax.ShapeDtypeStruct((dests, count // dests + height, lanes), near.dtype),
        in_specs=[HBM] * 3 + [VMEM],
        out_specs=VMEM,
        scratch_shapes=[
            pltpu.SMEM((count,), jnp.int32),
            pltpu.VMEM(near.shape, near.dtype),
            pltpu.VMEM(far.shape, far.dtype),
            pltpu.VMEM((2 * near.shape[0], lanes), jnp.float32),
            pltpu.VMEM((count, lanes), jnp.float32),
            pltpu.SemaphoreType.DMA((4,)),
        ],
        compiler_params=pltpu.CompilerParams(vmem_limit_bytes=16 * 2**20),
        name="gather_rows",
    )(*in_hbm(rows, near, far), extra)


def forward_kernel(near, *rest):
    sources, (x_out, part, part16, table, picked, *copied, sems) = rest[:5], rest[5:]
    copies = start_copies(zip(sources, copied), sems)
    rows, far, upstream, v_proj, u_proj = copied
    half, lanes = near.shape
    rank = v_proj.shape[0]
    table[:half] = near[...].astype(jnp.float32)
    copies[1].wait()
    table[half:] = far[...].astype(jnp.float32)
    copies[0].wait()
    pick_rows(rows, table, picked)
    for copy in copies[2:]:
        copy.wait()
    ones = jnp.ones((8, 3 * lanes), jnp.bfloat16)
    h_sum = jnp.zeros((rank, lanes), jnp.float32)
    d_sum = jnp.zeros((rank, lanes), jnp.float32)
    for k in range(half // CHUNK):
        here = slice(k * CHUNK, (k + 1) * CHUNK)
        x = picked[here, :]
        scaled = upstream[here, :].astype(jnp.float32) * x
        x16 = x.astype(jnp.bfloat16)
        x_out[here, :] = x16
        sums = dot_last(ones, jnp.concatenate(split3(scaled), axis=1))
        for j in range(CHUNK // 128):
            row = k * (CHUNK // 128) + j
            part[2 * rank + row : 2 * rank + row + 1, :] = sums[:1, j * 128 : (j + 1) * 128]
        h_sum += jnp.dot(v_proj[:, here], x16, preferred_element_type=jnp.float32)
        d_sum += jnp.dot(
            u_proj[:, here], scaled.astype(jnp.bfloat16), preferred_element_type=jnp.float32
        )
    part[:rank] = h_sum
    part[rank : 2 * rank] = d_sum
    part16[:rank] = h_sum.astype(jnp.bfloat16)
    part16[rank:] = d_sum.astype(jnp.bfloat16)


def ranks_kernel(part, other, ranks, message, total):
    rows = other.shape[0]
    rank = rows // 2
    value = part[:rows] + other[...].astype(jnp.float32)
    ranks[...] = value.astype(jnp.bfloat16)
    total[...] = value
    step = rank // 128
    for i in range(2):
        for j in range(step):
            to = i * rank + j * 128
            rank_rows = total[pl.ds(i * rank + j, 128, stride=step), :]
            message[to : to + 128, :] = rank_rows.astype(jnp.bfloat16)
    store3(message, rows, part[rows:])


def grads_kernel(place, x_group, up_group, *rest):
    *ranks, pieces, result, spread, bias_rows = rest
    count, wide, lanes = x_group.shape
    ny = count // 2
    y, c = place[0], place[1]
    rank = (ranks[0].shape[0] - 128) // 2
    for part in range(2):
        here = slice(part * rank, (part + 1) * rank)
        acc = jnp.zeros((rank, wide), jnp.float32)
        for k in range(ny):
            pair = lax.rem(y + ny - k, ny) * 2
            left = jnp.concatenate([ranks[k][here, :], ranks[ny + k][here, :]], axis=1)
            right = [x_group[pair + c], x_group[pair + 1 - c]]
            if part == 0:
                ups = [up_group[pair + c], up_group[pair + 1 - c]]
                right = [
                    (up.astype(jnp.float32) * x.astype(jnp.float32)).astype(jnp.bfloat16)
                    for up, x in zip(ups, right)
                ]
            acc = acc + dot_last(left, jnp.concatenate(right, axis=1))
        result[:, part * wide : (part + 1) * wide] = acc
    dests, height, _ = pieces.shape
    blocks = 2 * wide // lanes
    for j in range(rank // dests):
        for k in range(blocks):
            spread[pl.ds(j * blocks + k, dests, stride=height), :] = result[
                j * dests : (j + 1) * dests, k * lanes : (k + 1) * lanes
            ]
    bias_rows[...] = sum(join3(block[2 * rank :, :]) for block in ranks)
    mine = (y * 2 + c) * (wide // lanes)
    first = rank // dests * blocks
    for k in range(wide // lanes):
        row = bias_rows[pl.ds(mine + k, 1), :]
        high = row.astype(jnp.bfloat16).astype(jnp.float32)
        for i, value in enumerate((high, row - high)):
            at = first + i * (wide // lanes) + k
            spread[pl.ds(at, dests, stride=height), :] = jnp.broadcast_to(value, (dests, lanes))
    pieces[...] = spread[...].reshape(dests, height, lanes).astype(jnp.bfloat16)


def arrive_kernel(got, d_looked, grad_u, grad_v, grad_bias, *, block, wide, norm):
    sources, height, lanes = got.shape
    for k in range(sources):
        d_looked[:, k * lanes : (k + 1) * lanes] = got[k, :block, :]
    columns = wide // lanes
    group = grad_u.shape[1] // wide
    first = 2 * columns * grad_u.shape[0]
    for b in range(group):
        total = jnp.zeros((height - block, lanes), jnp.float32)
        for k in range(sources // group):
            total += got[k * group + b, block:, :].astype(jnp.float32)
        total = total * norm
        for k in range(columns):
            here = slice(b * wide + k * lanes, b * wide + (k + 1) * lanes)
            for j in range(grad_u.shape[0]):
                row = j * 2 * columns + k
                grad_u[j : j + 1, here] = total[row : row + 1]
                grad_v[j : j + 1, here] = total[row + columns : row + columns + 1]
            row = first + k
            grad_bias[b * columns + k : b * columns + k + 1, :] = (
                total[row : row + 1] + total[row + columns : row + columns + 1]
            )


def inverse_rows(column_owner, first_column, count):
    wires = jnp.arange(column_owner.shape[0], dtype=jnp.int32)
    high = column_owner // 128 - first_column // 128
    low = column_owner % 128
    pick = (high[None, :] == jnp.arange(count // 128, dtype=jnp.int32)[:, None]).astype(jnp.bfloat16)
    lanes = low[:, None] == jnp.arange(128, dtype=jnp.int32)[None, :]
    values = jnp.concatenate(
        [
            jnp.where(lanes, (wires // 128)[:, None].astype(jnp.bfloat16), 0),
            jnp.where(lanes, (wires % 128)[:, None].astype(jnp.bfloat16), 0),
        ],
        axis=1,
    )
    found = jnp.dot(pick, values, preferred_element_type=jnp.float32).astype(jnp.int32)
    return (found[:, :128] * 128 + found[:, 128:]).reshape(-1)


def step(looked, column_owner, v_proj, u_proj, bias, upstream):
    y, c, t = (lax.axis_index(a).astype(jnp.int32) for a in ("y", "c", "t"))
    ny = lax.axis_size("y")
    dp_count = lax.axis_size(DP)
    block_rows = looked.shape[0]
    rank, half_width = v_proj.shape
    samples = upstream.shape[1]
    norm = 1.0 / math.sqrt(samples * dp_count)
    bf16 = jnp.bfloat16

    array = jax.ShapeDtypeStruct
    group = 2 * ny
    wide = half_width // group
    arrived = lax.all_to_all(looked, DP, split_axis=1, concat_axis=0, tiled=True)
    partner = lax.ppermute(arrived, "t", SWAP)
    up_group = lax.all_to_all(
        upstream.reshape(group, wide, samples), ("y", "c"), split_axis=0, concat_axis=0, tiled=True
    )
    wire = inverse_rows(column_owner, t * half_width, half_width)
    side = wire // block_rows % 2
    spot = wire // (2 * block_rows) * block_rows + wire % block_rows
    x_rows = jnp.where(side == t, 0, half_width) + spot
    x_zero, part, part16 = local_call(
        forward_kernel,
        [
            array((half_width, samples), bf16),
            array((2 * rank + half_width // 128, samples), jnp.float32),
            array((2 * rank, samples), bf16),
        ],
        arrived,
        *in_hbm(x_rows, partner, upstream, v_proj, u_proj),
        scratch_shapes=[
            pltpu.VMEM((2 * half_width, samples), jnp.float32),
            pltpu.VMEM((half_width, samples), jnp.float32),
            pltpu.SMEM(x_rows.shape, jnp.int32),
            pltpu.VMEM(partner.shape, bf16),
            pltpu.VMEM(upstream.shape, bf16),
            pltpu.VMEM(v_proj.shape, bf16),
            pltpu.VMEM(u_proj.shape, bf16),
            pltpu.SemaphoreType.DMA((5,)),
        ],
        specs=[VMEM] + [HBM] * 5,
        mib=28,
    )
    other = lax.ppermute(part16, "t", SWAP)
    x_group = lax.all_to_all(
        x_zero.reshape(group, wide, samples), ("y", "c"), split_axis=0, concat_axis=0, tiled=True
    )
    ranks, message = local_call(
        ranks_kernel,
        [array((2 * rank, samples), bf16), array((2 * rank + 128, samples), bf16)],
        part,
        other,
        scratch_shapes=[pltpu.VMEM((2 * rank, samples), jnp.float32)],
        mib=4,
    )
    mix = dot_first(u_proj, ranks[:rank]) + bias[:, None]
    cotan = upstream.astype(jnp.float32)
    dx_zero = (cotan * (mix + 1.0) + dot_first(v_proj, ranks[rank:])).astype(bf16)
    dx_other = lax.ppermute(dx_zero, "t", SWAP)

    blocks = [message]
    for k in range(1, ny):
        blocks.append(shift(message, "y", ny, k))
    blocks = blocks + [lax.ppermute(block, "c", SWAP) for block in blocks]
    height = rank // dp_count * (2 * wide // 128) + 2 * wide // 128
    pieces = local_call(
        grads_kernel,
        array((dp_count, height, 128), bf16),
        jnp.stack([y, c]),
        x_group,
        up_group,
        *blocks,
        scalars=1,
        scratch_shapes=[
            pltpu.VMEM((rank, 2 * wide), jnp.float32),
            pltpu.VMEM((dp_count * height, 128), jnp.float32),
            pltpu.VMEM((32, 128), jnp.float32),
        ],
        mib=16,
    )

    columns = lax.dynamic_index_in_dim(
        column_owner.reshape(dp_count, 2, block_rows), t, 1, keepdims=False
    ).reshape(-1)
    out_rows = jnp.where(columns // half_width == t, 0, half_width) + columns % half_width
    outgoing = gather(out_rows, dx_zero, dx_other, pieces)
    got = lax.all_to_all(outgoing, DP, split_axis=0, concat_axis=0, tiled=True)
    d_looked, grad_u, grad_v, grad_bias = local_call(
        lambda *refs: arrive_kernel(*refs, block=block_rows, wide=wide, norm=norm),
        [
            array((block_rows, dp_count * samples), bf16),
            array((rank // dp_count, half_width), jnp.float32),
            array((rank // dp_count, half_width), jnp.float32),
            array((half_width // 128, 128), jnp.float32),
        ],
        got,
        mib=8,
    )
    return (d_looked, grad_u, grad_v, grad_bias.reshape(-1))


def solution(mesh):
    fine = Mesh(mesh.devices.reshape(8, 2, 4, 2, 2), DP + ("t",))
    in_specs = (
        P(DP + ("t",), None),
        P(),
        P(None, "t"),
        P(None, "t"),
        P("t"),
        P("t", DP),
    )
    out_specs = (P(DP + ("t",), None), P(DP, "t"), P(DP, "t"), P("t"))
    return jax.shard_map(step, mesh=fine, in_specs=in_specs, out_specs=out_specs, check_vma=False)
```

```python
import math

import jax
import jax.numpy as jnp
from jax import lax
from jax.experimental import pallas as pl
from jax.experimental.pallas import tpu as pltpu
from jax.sharding import Mesh, PartitionSpec as P


DP = ("z", "xl", "y", "c")
SWAP = [(0, 1), (1, 0)]
UNROLL = 32
CHUNK = 512


SMEM = pl.BlockSpec(memory_space=pltpu.SMEM)
VMEM = pl.BlockSpec(memory_space=pltpu.VMEM)
HBM = pl.BlockSpec(memory_space=pltpu.HBM)


def dot_last(left, right):
    return lax.dot_general(
        left, right, (((1,), (1,)), ((), ())), preferred_element_type=jnp.float32
    )


def dot_first(left, right):
    return lax.dot_general(
        left, right, (((0,), (0,)), ((), ())), preferred_element_type=jnp.float32
    )


def shift(value, axis, size, by):
    return lax.ppermute(value, axis, [(i, (i + by) % size) for i in range(size)])


def split3(value):
    high = value.astype(jnp.bfloat16)
    rest = value - high.astype(jnp.float32)
    middle = rest.astype(jnp.bfloat16)
    low = (rest - middle.astype(jnp.float32)).astype(jnp.bfloat16)
    return high, middle, low


def join3(parts):
    rows = parts.shape[0] // 4
    wide = parts.astype(jnp.float32)
    return wide[:rows] + wide[rows : 2 * rows] + wide[2 * rows : 3 * rows]


def store3(out, start, value):
    rows = value.shape[0]
    for i, part in enumerate(split3(value)):
        out[start + i * rows : start + (i + 1) * rows, :] = part
    out[start + 3 * rows : start + 4 * rows, :] = jnp.zeros((rows, value.shape[1]), jnp.bfloat16)


def local_call(body, out_shape, *args, scalars=0, mib, specs=None, **kwargs):
    return pl.pallas_call(
        body,
        out_shape=out_shape,
        in_specs=specs or [SMEM] * scalars + [VMEM] * (len(args) - scalars),
        out_specs=jax.tree.map(lambda _: VMEM, out_shape),
        compiler_params=pltpu.CompilerParams(vmem_limit_bytes=mib * 2**20),
        **kwargs,
    )(*args)


def pick_rows(rows, table, picked):
    def step(i, carry):
        for j in range(UNROLL):
            k = i * UNROLL + j
            picked[pl.ds(k, 1), :] = table[pl.ds(rows[k], 1), :]
        return carry

    lax.fori_loop(0, picked.shape[0] // UNROLL, step, 0)


def gather_kernel(rows, near, far, extra, out, table, picked):
    half = near.shape[0]
    dests, height, lanes = out.shape
    block = height - extra.shape[1]
    table[:half] = near[...].astype(jnp.float32)
    table[half:] = far[...].astype(jnp.float32)
    pick_rows(rows, table, picked)
    out[:, :block, :] = picked[...].reshape(dests, block, lanes).astype(out.dtype)
    out[:, block:, :] = extra[...]


def gather(rows, near, far, extra):
    count, lanes = rows.shape[0], near.shape[1]
    dests, height, _ = extra.shape
    return pl.pallas_call(
        gather_kernel,
        out_shape=jax.ShapeDtypeStruct((dests, count // dests + height, lanes), near.dtype),
        in_specs=[SMEM, VMEM, VMEM, VMEM],
        out_specs=VMEM,
        scratch_shapes=[
            pltpu.VMEM((2 * near.shape[0], lanes), jnp.float32),
            pltpu.VMEM((count, lanes), jnp.float32),
        ],
        compiler_params=pltpu.CompilerParams(vmem_limit_bytes=16 * 2**20),
        name="gather_rows",
    )(rows, near, far, extra)


def start_copies(pairs, sems):
    copies = [pltpu.make_async_copy(a, b, sems.at[i]) for i, (a, b) in enumerate(pairs)]
    for copy in copies:
        copy.start()
    return copies


def in_hbm(*values):
    return [pltpu.with_memory_space_constraint(value, pltpu.HBM) for value in values]


def forward_kernel(near, *rest):
    sources, (x_out, part, part16, table, picked, *copied, sems) = rest[:5], rest[5:]
    copies = start_copies(zip(sources, copied), sems)
    rows, far, upstream, v_proj, u_proj = copied
    half, lanes = near.shape
    rank = v_proj.shape[0]
    table[:half] = near[...].astype(jnp.float32)
    copies[1].wait()
    table[half:] = far[...].astype(jnp.float32)
    copies[0].wait()
    pick_rows(rows, table, picked)
    for copy in copies[2:]:
        copy.wait()
    ones = jnp.ones((8, 3 * lanes), jnp.bfloat16)
    h_sum = jnp.zeros((rank, lanes), jnp.float32)
    d_sum = jnp.zeros((rank, lanes), jnp.float32)
    for k in range(half // CHUNK):
        here = slice(k * CHUNK, (k + 1) * CHUNK)
        x = picked[here, :]
        scaled = upstream[here, :].astype(jnp.float32) * x
        x16 = x.astype(jnp.bfloat16)
        x_out[here, :] = x16
        sums = dot_last(ones, jnp.concatenate(split3(scaled), axis=1))
        for j in range(CHUNK // 128):
            row = k * (CHUNK // 128) + j
            part[2 * rank + row : 2 * rank + row + 1, :] = sums[:1, j * 128 : (j + 1) * 128]
        h_sum += jnp.dot(v_proj[:, here], x16, preferred_element_type=jnp.float32)
        d_sum += jnp.dot(
            u_proj[:, here], scaled.astype(jnp.bfloat16), preferred_element_type=jnp.float32
        )
    part[:rank] = h_sum
    part[rank : 2 * rank] = d_sum
    part16[:rank] = h_sum.astype(jnp.bfloat16)
    part16[rank:] = d_sum.astype(jnp.bfloat16)


def ranks_kernel(part, other, ranks, message, total):
    rows = other.shape[0]
    value = part[:rows] + other[...].astype(jnp.float32)
    ranks[...] = value.astype(jnp.bfloat16)
    total[...] = value
    step = rows // 2 // 128
    for i in range(2):
        for j in range(step):
            to = i * rows // 2 + j * 128
            rank_rows = total[pl.ds(i * rows // 2 + j, 128, stride=step), :]
            message[to : to + 128, :] = rank_rows.astype(jnp.bfloat16)
    store3(message, rows, part[rows:])


def join_kernel(*rest):
    *blocks, message = rest
    rows = (message.shape[0] - 128) // len(blocks)
    bias = jnp.zeros((32, 128), jnp.float32)
    for k, block in enumerate(blocks):
        message[k * rows : (k + 1) * rows, :] = block[:rows, :]
        bias += join3(block[rows:, :])
    store3(message, len(blocks) * rows, bias)


def join_blocks(blocks):
    rows, lanes = blocks[0].shape
    shape = jax.ShapeDtypeStruct(((rows - 128) * len(blocks) + 128, lanes), blocks[0].dtype)
    return local_call(join_kernel, shape, *blocks, mib=6)


def grads_kernel(place, x_group, up_group, near_ranks, far_ranks, pieces, result, spread, bias_rows):
    count, wide, lanes = x_group.shape
    ny = count // 2
    y, c = place[0], place[1]
    both = near_ranks.shape[0] // ny // 128 * 128
    rank = both // 2
    for part in range(2):
        acc = jnp.zeros((rank, wide), jnp.float32)
        for k in range(ny):
            here = slice(k * both + part * rank, k * both + (part + 1) * rank)
            pair = lax.rem(y + ny - k, ny) * 2
            left = jnp.concatenate([near_ranks[here, :], far_ranks[here, :]], axis=1)
            right = [x_group[pair + c], x_group[pair + 1 - c]]
            if part == 0:
                ups = [up_group[pair + c], up_group[pair + 1 - c]]
                right = [
                    (up.astype(jnp.float32) * x.astype(jnp.float32)).astype(jnp.bfloat16)
                    for up, x in zip(ups, right)
                ]
            acc = acc + dot_last(left, jnp.concatenate(right, axis=1))
        result[:, part * wide : (part + 1) * wide] = acc
    dests, height, _ = pieces.shape
    blocks = 2 * wide // lanes
    for j in range(rank // dests):
        for k in range(blocks):
            spread[pl.ds(j * blocks + k, dests, stride=height), :] = result[
                j * dests : (j + 1) * dests, k * lanes : (k + 1) * lanes
            ]
    bias = join3(near_ranks[ny * both :, :]) + join3(far_ranks[ny * both :, :])
    bias_rows[...] = bias
    mine = (y * 2 + c) * (wide // lanes)
    first = rank // dests * blocks
    for k in range(wide // lanes):
        row = bias_rows[pl.ds(mine + k, 1), :]
        high = row.astype(jnp.bfloat16).astype(jnp.float32)
        for i, value in enumerate((high, row - high)):
            at = first + i * (wide // lanes) + k
            spread[pl.ds(at, dests, stride=height), :] = jnp.broadcast_to(value, (dests, lanes))
    pieces[...] = spread[...].reshape(dests, height, lanes).astype(jnp.bfloat16)


def arrive_kernel(got, d_looked, grad_u, grad_v, grad_bias, *, block, wide, norm):
    sources, height, lanes = got.shape
    for k in range(sources):
        d_looked[:, k * lanes : (k + 1) * lanes] = got[k, :block, :]
    columns = wide // lanes
    group = grad_u.shape[1] // wide
    first = 2 * columns * grad_u.shape[0]
    for b in range(group):
        total = jnp.zeros((height - block, lanes), jnp.float32)
        for k in range(sources // group):
            total += got[k * group + b, block:, :].astype(jnp.float32)
        total = total * norm
        for k in range(columns):
            here = slice(b * wide + k * lanes, b * wide + (k + 1) * lanes)
            for j in range(grad_u.shape[0]):
                row = j * 2 * columns + k
                grad_u[j : j + 1, here] = total[row : row + 1]
                grad_v[j : j + 1, here] = total[row + columns : row + columns + 1]
            row = first + k
            grad_bias[b * columns + k : b * columns + k + 1, :] = (
                total[row : row + 1] + total[row + columns : row + columns + 1]
            )


def inverse_rows(column_owner, first_column, count):
    wires = jnp.arange(column_owner.shape[0], dtype=jnp.int32)
    high = column_owner // 128 - first_column // 128
    low = column_owner % 128
    pick = (high[None, :] == jnp.arange(count // 128, dtype=jnp.int32)[:, None]).astype(jnp.bfloat16)
    lanes = low[:, None] == jnp.arange(128, dtype=jnp.int32)[None, :]
    values = jnp.concatenate(
        [
            jnp.where(lanes, (wires // 128)[:, None].astype(jnp.bfloat16), 0),
            jnp.where(lanes, (wires % 128)[:, None].astype(jnp.bfloat16), 0),
        ],
        axis=1,
    )
    found = jnp.dot(pick, values, preferred_element_type=jnp.float32).astype(jnp.int32)
    return (found[:, :128] * 128 + found[:, 128:]).reshape(-1)


def step(looked, column_owner, v_proj, u_proj, bias, upstream):
    y, c, t = (lax.axis_index(a).astype(jnp.int32) for a in ("y", "c", "t"))
    ny = lax.axis_size("y")
    dp_count = lax.axis_size(DP)
    block_rows = looked.shape[0]
    rank, half_width = v_proj.shape
    samples = upstream.shape[1]
    norm = 1.0 / math.sqrt(samples * dp_count)
    bf16 = jnp.bfloat16

    array = jax.ShapeDtypeStruct
    group = 2 * ny
    wide = half_width // group
    arrived = lax.all_to_all(looked, DP, split_axis=1, concat_axis=0, tiled=True)
    partner = lax.ppermute(arrived, "t", SWAP)
    up_group = lax.all_to_all(
        upstream.reshape(group, wide, samples), ("y", "c"), split_axis=0, concat_axis=0, tiled=True
    )
    wire = inverse_rows(column_owner, t * half_width, half_width)
    side = wire // block_rows % 2
    spot = wire // (2 * block_rows) * block_rows + wire % block_rows
    x_rows = jnp.where(side == t, 0, half_width) + spot
    x_zero, part, part16 = local_call(
        forward_kernel,
        [
            array((half_width, samples), bf16),
            array((2 * rank + half_width // 128, samples), jnp.float32),
            array((2 * rank, samples), bf16),
        ],
        arrived,
        *in_hbm(x_rows, partner, upstream, v_proj, u_proj),
        scratch_shapes=[
            pltpu.VMEM((2 * half_width, samples), jnp.float32),
            pltpu.VMEM((half_width, samples), jnp.float32),
            pltpu.SMEM(x_rows.shape, jnp.int32),
            pltpu.VMEM(partner.shape, bf16),
            pltpu.VMEM(upstream.shape, bf16),
            pltpu.VMEM(v_proj.shape, bf16),
            pltpu.VMEM(u_proj.shape, bf16),
            pltpu.SemaphoreType.DMA((5,)),
        ],
        specs=[VMEM] + [HBM] * 5,
        mib=28,
    )
    other = lax.ppermute(part16, "t", SWAP)
    x_group = lax.all_to_all(
        x_zero.reshape(group, wide, samples), ("y", "c"), split_axis=0, concat_axis=0, tiled=True
    )
    ranks, message = local_call(
        ranks_kernel,
        [array((2 * rank, samples), bf16), array((2 * rank + 128, samples), bf16)],
        part,
        other,
        scratch_shapes=[pltpu.VMEM((2 * rank, samples), jnp.float32)],
        mib=4,
    )

    mix = dot_first(u_proj, ranks[:rank]) + bias[:, None]
    cotan = upstream.astype(jnp.float32)
    dx_zero = (cotan * (mix + 1.0) + dot_first(v_proj, ranks[rank:])).astype(bf16)
    dx_other = lax.ppermute(dx_zero, "t", SWAP)

    blocks = [message]
    for k in range(1, ny):
        blocks.append(shift(blocks[0], "y", ny, k))
    near_ranks = join_blocks(blocks)
    far_ranks = lax.ppermute(near_ranks, "c", SWAP)
    height = rank // dp_count * (2 * wide // 128) + 2 * wide // 128
    pieces = local_call(
        grads_kernel,
        array((dp_count, height, 128), bf16),
        jnp.stack([y, c]),
        x_group,
        up_group,
        near_ranks,
        far_ranks,
        scalars=1,
        scratch_shapes=[
            pltpu.VMEM((rank, 2 * wide), jnp.float32),
            pltpu.VMEM((dp_count * height, 128), jnp.float32),
            pltpu.VMEM((32, 128), jnp.float32),
        ],
        mib=16,
    )

    columns = lax.dynamic_index_in_dim(
        column_owner.reshape(dp_count, 2, block_rows), t, 1, keepdims=False
    ).reshape(-1)
    out_rows = jnp.where(columns // half_width == t, 0, half_width) + columns % half_width
    outgoing = gather(out_rows, dx_zero, dx_other, pieces)
    got = lax.all_to_all(outgoing, DP, split_axis=0, concat_axis=0, tiled=True)
    d_looked, grad_u, grad_v, grad_bias = local_call(
        lambda *refs: arrive_kernel(*refs, block=block_rows, wide=wide, norm=norm),
        [
            array((block_rows, dp_count * samples), bf16),
            array((rank // dp_count, half_width), jnp.float32),
            array((rank // dp_count, half_width), jnp.float32),
            array((half_width // 128, 128), jnp.float32),
        ],
        got,
        mib=8,
    )
    return (d_looked, grad_u, grad_v, grad_bias.reshape(-1))


def solution(mesh):
    fine = Mesh(mesh.devices.reshape(8, 2, 4, 2, 2), DP + ("t",))
    in_specs = (
        P(DP + ("t",), None),
        P(),
        P(None, "t"),
        P(None, "t"),
        P("t"),
        P("t", DP),
    )
    out_specs = (P(DP + ("t",), None), P(DP, "t"), P(DP, "t"), P("t"))
    return jax.shard_map(step, mesh=fine, in_specs=in_specs, out_specs=out_specs, check_vma=False)
```

```python
import math

import jax
import jax.numpy as jnp
from jax import lax
from jax.experimental import pallas as pl
from jax.experimental.pallas import tpu as pltpu
from jax.sharding import Mesh, PartitionSpec as P


DP = ("z", "xl", "y", "c")
SWAP = [(0, 1), (1, 0)]
UNROLL = 32
CHUNK = 512


SMEM = pl.BlockSpec(memory_space=pltpu.SMEM)
VMEM = pl.BlockSpec(memory_space=pltpu.VMEM)
HBM = pl.BlockSpec(memory_space=pltpu.HBM)


def dot_last(left, right):
    return lax.dot_general(
        left, right, (((1,), (1,)), ((), ())), preferred_element_type=jnp.float32
    )


def dot_first(left, right):
    return lax.dot_general(
        left, right, (((0,), (0,)), ((), ())), preferred_element_type=jnp.float32
    )


def shift(value, axis, size, by):
    return lax.ppermute(value, axis, [(i, (i + by) % size) for i in range(size)])


def split3(value):
    high = value.astype(jnp.bfloat16)
    rest = value - high.astype(jnp.float32)
    middle = rest.astype(jnp.bfloat16)
    low = (rest - middle.astype(jnp.float32)).astype(jnp.bfloat16)
    return high, middle, low


def join3(parts):
    rows = parts.shape[0] // 4
    wide = parts.astype(jnp.float32)
    return wide[:rows] + wide[rows : 2 * rows] + wide[2 * rows : 3 * rows]


def store3(out, start, value):
    rows = value.shape[0]
    for i, part in enumerate(split3(value)):
        out[start + i * rows : start + (i + 1) * rows, :] = part
    out[start + 3 * rows : start + 4 * rows, :] = jnp.zeros((rows, value.shape[1]), jnp.bfloat16)


def local_call(body, out_shape, *args, scalars=0, mib, specs=None, outs=None, **kwargs):
    return pl.pallas_call(
        body,
        out_shape=out_shape,
        in_specs=specs or [SMEM] * scalars + [VMEM] * (len(args) - scalars),
        out_specs=outs or jax.tree.map(lambda _: VMEM, out_shape),
        compiler_params=pltpu.CompilerParams(vmem_limit_bytes=mib * 2**20),
        **kwargs,
    )(*args)


def pick_rows(rows, table, picked):
    def step(i, carry):
        for j in range(UNROLL):
            k = i * UNROLL + j
            picked[pl.ds(k, 1), :] = table[pl.ds(rows[k], 1), :]
        return carry

    lax.fori_loop(0, picked.shape[0] // UNROLL, step, 0)


def gather_kernel(rows_in, near, far_in, extra, out, rows, far, table, picked, sems):
    half = near.shape[0]
    dests, height, lanes = out.shape
    block = height - extra.shape[1]
    copies = start_copies(((far_in, far), (rows_in, rows), (extra, out.at[:, block:, :])), sems)
    table[:half] = near[...].astype(jnp.float32)
    copies[0].wait()
    table[half:] = far[...].astype(jnp.float32)
    copies[1].wait()
    pick_rows(rows, table, picked)
    out[:, :block, :] = picked[...].reshape(dests, block, lanes).astype(out.dtype)
    copies[2].wait()


def gather(rows, near, far, extra):
    count, lanes = rows.shape[0], near.shape[1]
    dests, height, _ = extra.shape
    rows, far = in_hbm(rows, far)
    return pl.pallas_call(
        gather_kernel,
        out_shape=jax.ShapeDtypeStruct((dests, count // dests + height, lanes), near.dtype),
        in_specs=[HBM, VMEM, HBM, VMEM],
        out_specs=VMEM,
        scratch_shapes=[
            pltpu.SMEM((count,), jnp.int32),
            pltpu.VMEM(near.shape, near.dtype),
            pltpu.VMEM((2 * near.shape[0], lanes), jnp.float32),
            pltpu.VMEM((count, lanes), jnp.float32),
            pltpu.SemaphoreType.DMA((3,)),
        ],
        compiler_params=pltpu.CompilerParams(vmem_limit_bytes=16 * 2**20),
        name="gather_rows",
    )(rows, near, far, extra)


def start_copies(pairs, sems):
    copies = [pltpu.make_async_copy(a, b, sems.at[i]) for i, (a, b) in enumerate(pairs)]
    for copy in copies:
        copy.start()
    return copies


def in_hbm(*values):
    return [pltpu.with_memory_space_constraint(value, pltpu.HBM) for value in values]


def forward_kernel(near, *rest):
    sources, (x_out, part, part16, table, picked, *copied, sems) = rest[:5], rest[5:]
    copies = start_copies(zip(sources, copied), sems)
    rows, far, upstream, v_proj, u_proj, staged = copied
    sent = []
    half, lanes = near.shape
    rank = v_proj.shape[0]
    table[:half] = near[...].astype(jnp.float32)
    copies[1].wait()
    table[half:] = far[...].astype(jnp.float32)
    copies[0].wait()
    pick_rows(rows, table, picked)
    for copy in copies[2:]:
        copy.wait()
    ones = jnp.ones((8, 3 * lanes), jnp.bfloat16)
    h_sum = jnp.zeros((rank, lanes), jnp.float32)
    d_sum = jnp.zeros((rank, lanes), jnp.float32)
    for k in range(half // CHUNK):
        here = slice(k * CHUNK, (k + 1) * CHUNK)
        x = picked[here, :]
        scaled = upstream[here, :].astype(jnp.float32) * x
        x16 = x.astype(jnp.bfloat16)
        staged[here, :] = x16
        sent.append(pltpu.make_async_copy(staged.at[here], x_out.at[here], sems.at[5 + k]))
        sent[-1].start()
        sums = dot_last(ones, jnp.concatenate(split3(scaled), axis=1))
        for j in range(CHUNK // 128):
            row = k * (CHUNK // 128) + j
            part[2 * rank + row : 2 * rank + row + 1, :] = sums[:1, j * 128 : (j + 1) * 128]
        h_sum += jnp.dot(v_proj[:, here], x16, preferred_element_type=jnp.float32)
        d_sum += jnp.dot(
            u_proj[:, here], scaled.astype(jnp.bfloat16), preferred_element_type=jnp.float32
        )
    part[:rank] = h_sum
    part[rank : 2 * rank] = d_sum
    part16[:rank] = h_sum.astype(jnp.bfloat16)
    part16[rank:] = d_sum.astype(jnp.bfloat16)
    for copy in sent:
        copy.wait()


def ranks_kernel(part, other, ranks, message, total):
    rows = other.shape[0]
    value = part[:rows] + other[...].astype(jnp.float32)
    ranks[...] = value.astype(jnp.bfloat16)
    total[...] = value
    step = rows // 2 // 128
    for i in range(2):
        for j in range(step):
            to = i * rows // 2 + j * 128
            rank_rows = total[pl.ds(i * rows // 2 + j, 128, stride=step), :]
            message[to : to + 128, :] = rank_rows.astype(jnp.bfloat16)
    store3(message, rows, part[rows:])


def join_kernel(*rest):
    *blocks, message = rest
    rows = (message.shape[0] - 128) // len(blocks)
    bias = jnp.zeros((32, 128), jnp.float32)
    for k, block in enumerate(blocks):
        message[k * rows : (k + 1) * rows, :] = block[:rows, :]
        bias += join3(block[rows:, :])
    store3(message, len(blocks) * rows, bias)


def join_blocks(blocks):
    rows, lanes = blocks[0].shape
    shape = jax.ShapeDtypeStruct(((rows - 128) * len(blocks) + 128, lanes), blocks[0].dtype)
    return local_call(join_kernel, shape, *blocks, mib=6)


def grads_kernel(place, x_group, up_group, near_ranks, far_ranks, pieces, result, spread, bias_rows):
    count, wide, lanes = x_group.shape
    ny = count // 2
    y, c = place[0], place[1]
    both = near_ranks.shape[0] // ny // 128 * 128
    rank = both // 2
    for part in range(2):
        acc = jnp.zeros((rank, wide), jnp.float32)
        for k in range(ny):
            here = slice(k * both + part * rank, k * both + (part + 1) * rank)
            pair = lax.rem(y + ny - k, ny) * 2
            left = jnp.concatenate([near_ranks[here, :], far_ranks[here, :]], axis=1)
            right = [x_group[pair + c], x_group[pair + 1 - c]]
            if part == 0:
                ups = [up_group[pair + c], up_group[pair + 1 - c]]
                right = [
                    (up.astype(jnp.float32) * x.astype(jnp.float32)).astype(jnp.bfloat16)
                    for up, x in zip(ups, right)
                ]
            acc = acc + dot_last(left, jnp.concatenate(right, axis=1))
        result[:, part * wide : (part + 1) * wide] = acc
    dests, height, _ = pieces.shape
    blocks = 2 * wide // lanes
    for j in range(rank // dests):
        for k in range(blocks):
            spread[pl.ds(j * blocks + k, dests, stride=height), :] = result[
                j * dests : (j + 1) * dests, k * lanes : (k + 1) * lanes
            ]
    bias = join3(near_ranks[ny * both :, :]) + join3(far_ranks[ny * both :, :])
    bias_rows[...] = bias
    mine = (y * 2 + c) * (wide // lanes)
    first = rank // dests * blocks
    for k in range(wide // lanes):
        row = bias_rows[pl.ds(mine + k, 1), :]
        high = row.astype(jnp.bfloat16).astype(jnp.float32)
        for i, value in enumerate((high, row - high)):
            at = first + i * (wide // lanes) + k
            spread[pl.ds(at, dests, stride=height), :] = jnp.broadcast_to(value, (dests, lanes))
    pieces[...] = spread[...].reshape(dests, height, lanes).astype(jnp.bfloat16)


def arrive_kernel(got, d_looked, grad_u, grad_v, grad_bias, *, block, wide, norm):
    sources, height, lanes = got.shape
    for k in range(sources):
        d_looked[:, k * lanes : (k + 1) * lanes] = got[k, :block, :]
    columns = wide // lanes
    group = grad_u.shape[1] // wide
    first = 2 * columns * grad_u.shape[0]
    for b in range(group):
        total = jnp.zeros((height - block, lanes), jnp.float32)
        for k in range(sources // group):
            total += got[k * group + b, block:, :].astype(jnp.float32)
        total = total * norm
        for k in range(columns):
            here = slice(b * wide + k * lanes, b * wide + (k + 1) * lanes)
            for j in range(grad_u.shape[0]):
                row = j * 2 * columns + k
                grad_u[j : j + 1, here] = total[row : row + 1]
                grad_v[j : j + 1, here] = total[row + columns : row + columns + 1]
            row = first + k
            grad_bias[b * columns + k : b * columns + k + 1, :] = (
                total[row : row + 1] + total[row + columns : row + columns + 1]
            )


def inverse_rows(column_owner, first_column, count):
    wires = jnp.arange(column_owner.shape[0], dtype=jnp.int32)
    high = column_owner // 128 - first_column // 128
    low = column_owner % 128
    pick = (high[None, :] == jnp.arange(count // 128, dtype=jnp.int32)[:, None]).astype(jnp.bfloat16)
    lanes = low[:, None] == jnp.arange(128, dtype=jnp.int32)[None, :]
    values = jnp.concatenate(
        [
            jnp.where(lanes, (wires // 128)[:, None].astype(jnp.bfloat16), 0),
            jnp.where(lanes, (wires % 128)[:, None].astype(jnp.bfloat16), 0),
        ],
        axis=1,
    )
    found = jnp.dot(pick, values, preferred_element_type=jnp.float32).astype(jnp.int32)
    return (found[:, :128] * 128 + found[:, 128:]).reshape(-1)


def step(looked, column_owner, v_proj, u_proj, bias, upstream):
    y, c, t = (lax.axis_index(a).astype(jnp.int32) for a in ("y", "c", "t"))
    ny = lax.axis_size("y")
    dp_count = lax.axis_size(DP)
    block_rows = looked.shape[0]
    rank, half_width = v_proj.shape
    samples = upstream.shape[1]
    norm = 1.0 / math.sqrt(samples * dp_count)
    bf16 = jnp.bfloat16

    array = jax.ShapeDtypeStruct
    group = 2 * ny
    wide = half_width // group
    arrived = lax.all_to_all(looked, DP, split_axis=1, concat_axis=0, tiled=True)
    partner = lax.ppermute(arrived, "t", SWAP)
    up_group = lax.all_to_all(
        upstream.reshape(group, wide, samples), ("y", "c"), split_axis=0, concat_axis=0, tiled=True
    )
    wire = inverse_rows(column_owner, t * half_width, half_width)
    side = wire // block_rows % 2
    spot = wire // (2 * block_rows) * block_rows + wire % block_rows
    x_rows = jnp.where(side == t, 0, half_width) + spot
    x_zero, part, part16 = local_call(
        forward_kernel,
        [
            array((half_width, samples), bf16),
            array((2 * rank + half_width // 128, samples), jnp.float32),
            array((2 * rank, samples), bf16),
        ],
        arrived,
        *in_hbm(x_rows, partner, upstream, v_proj, u_proj),
        scratch_shapes=[
            pltpu.VMEM((2 * half_width, samples), jnp.float32),
            pltpu.VMEM((half_width, samples), jnp.float32),
            pltpu.SMEM(x_rows.shape, jnp.int32),
            pltpu.VMEM(partner.shape, bf16),
            pltpu.VMEM(upstream.shape, bf16),
            pltpu.VMEM(v_proj.shape, bf16),
            pltpu.VMEM(u_proj.shape, bf16),
            pltpu.VMEM(upstream.shape, bf16),
            pltpu.SemaphoreType.DMA((5 + half_width // CHUNK,)),
        ],
        specs=[VMEM] + [HBM] * 5,
        outs=[HBM, VMEM, VMEM],
        input_output_aliases={2: 0},
        mib=28,
    )
    other = lax.ppermute(part16, "t", SWAP)
    x_group = lax.all_to_all(
        x_zero.reshape(group, wide, samples), ("y", "c"), split_axis=0, concat_axis=0, tiled=True
    )
    ranks, message = local_call(
        ranks_kernel,
        [array((2 * rank, samples), bf16), array((2 * rank + 128, samples), bf16)],
        part,
        other,
        scratch_shapes=[pltpu.VMEM((2 * rank, samples), jnp.float32)],
        mib=4,
    )

    mix = dot_first(u_proj, ranks[:rank]) + bias[:, None]
    cotan = upstream.astype(jnp.float32)
    dx_zero = (cotan * (mix + 1.0) + dot_first(v_proj, ranks[rank:])).astype(bf16)
    dx_other = lax.ppermute(dx_zero, "t", SWAP)

    blocks = [message]
    for k in range(1, ny):
        blocks.append(shift(blocks[0], "y", ny, k))
    near_ranks = join_blocks(blocks)
    far_ranks = lax.ppermute(near_ranks, "c", SWAP)
    height = rank // dp_count * (2 * wide // 128) + 2 * wide // 128
    pieces = local_call(
        grads_kernel,
        array((dp_count, height, 128), bf16),
        jnp.stack([y, c]),
        x_group,
        up_group,
        near_ranks,
        far_ranks,
        scalars=1,
        scratch_shapes=[
            pltpu.VMEM((rank, 2 * wide), jnp.float32),
            pltpu.VMEM((dp_count * height, 128), jnp.float32),
            pltpu.VMEM((32, 128), jnp.float32),
        ],
        mib=16,
    )

    columns = lax.dynamic_index_in_dim(
        column_owner.reshape(dp_count, 2, block_rows), t, 1, keepdims=False
    ).reshape(-1)
    out_rows = jnp.where(columns // half_width == t, 0, half_width) + columns % half_width
    outgoing = gather(out_rows, dx_zero, dx_other, pieces)
    got = lax.all_to_all(outgoing, DP, split_axis=0, concat_axis=0, tiled=True)
    d_looked, grad_u, grad_v, grad_bias = local_call(
        lambda *refs: arrive_kernel(*refs, block=block_rows, wide=wide, norm=norm),
        [
            array((block_rows, dp_count * samples), bf16),
            array((rank // dp_count, half_width), jnp.float32),
            array((rank // dp_count, half_width), jnp.float32),
            array((half_width // 128, 128), jnp.float32),
        ],
        got,
        mib=8,
    )
    return (d_looked, grad_u, grad_v, grad_bias.reshape(-1))


def solution(mesh):
    fine = Mesh(mesh.devices.reshape(8, 2, 4, 2, 2), DP + ("t",))
    in_specs = (
        P(DP + ("t",), None),
        P(),
        P(None, "t"),
        P(None, "t"),
        P("t"),
        P("t", DP),
    )
    out_specs = (P(DP + ("t",), None), P(DP, "t"), P(DP, "t"), P("t"))
    return jax.shard_map(step, mesh=fine, in_specs=in_specs, out_specs=out_specs, check_vma=False)
```

```python
import math

import jax
import jax.numpy as jnp
from jax import lax
from jax.experimental import pallas as pl
from jax.experimental.pallas import tpu as pltpu
from jax.sharding import Mesh, PartitionSpec as P


DP = ("z", "xl", "y", "c")
SWAP = [(0, 1), (1, 0)]
UNROLL = 32
CHUNK = 512


SMEM = pl.BlockSpec(memory_space=pltpu.SMEM)
VMEM = pl.BlockSpec(memory_space=pltpu.VMEM)
HBM = pl.BlockSpec(memory_space=pltpu.HBM)


def dot_last(left, right):
    return lax.dot_general(
        left, right, (((1,), (1,)), ((), ())), preferred_element_type=jnp.float32
    )


def dot_first(left, right):
    return lax.dot_general(
        left, right, (((0,), (0,)), ((), ())), preferred_element_type=jnp.float32
    )


def shift(value, axis, size, by):
    return lax.ppermute(value, axis, [(i, (i + by) % size) for i in range(size)])


def split3(value):
    high = value.astype(jnp.bfloat16)
    rest = value - high.astype(jnp.float32)
    middle = rest.astype(jnp.bfloat16)
    low = (rest - middle.astype(jnp.float32)).astype(jnp.bfloat16)
    return high, middle, low


def local_call(body, out_shape, *args, scalars=0, mib, specs=None, outs=None, **kwargs):
    return pl.pallas_call(
        body,
        out_shape=out_shape,
        in_specs=specs or [SMEM] * scalars + [VMEM] * (len(args) - scalars),
        out_specs=outs or jax.tree.map(lambda _: VMEM, out_shape),
        compiler_params=pltpu.CompilerParams(vmem_limit_bytes=mib * 2**20),
        **kwargs,
    )(*args)


def pick_rows(rows, table, picked):
    def step(i, carry):
        for j in range(UNROLL):
            k = i * UNROLL + j
            picked[pl.ds(k, 1), :] = table[pl.ds(rows[k], 1), :]
        return carry

    lax.fori_loop(0, picked.shape[0] // UNROLL, step, 0)


def gather_kernel(rows_in, near, far_in, extra, out, rows, far, table, picked, sems):
    half = near.shape[0]
    dests, height, lanes = out.shape
    block = height - extra.shape[1]
    copies = start_copies(((far_in, far), (rows_in, rows), (extra, out.at[:, block:, :])), sems)
    table[:half] = near[...].astype(jnp.float32)
    copies[0].wait()
    table[half:] = far[...].astype(jnp.float32)
    copies[1].wait()
    pick_rows(rows, table, picked)
    out[:, :block, :] = picked[...].reshape(dests, block, lanes).astype(out.dtype)
    copies[2].wait()


def gather(rows, near, far, extra):
    count, lanes = rows.shape[0], near.shape[1]
    dests, height, _ = extra.shape
    rows, far = in_hbm(rows, far)
    return pl.pallas_call(
        gather_kernel,
        out_shape=jax.ShapeDtypeStruct((dests, count // dests + height, lanes), near.dtype),
        in_specs=[HBM, VMEM, HBM, VMEM],
        out_specs=VMEM,
        scratch_shapes=[
            pltpu.SMEM((count,), jnp.int32),
            pltpu.VMEM(near.shape, near.dtype),
            pltpu.VMEM((2 * near.shape[0], lanes), jnp.float32),
            pltpu.VMEM((count, lanes), jnp.float32),
            pltpu.SemaphoreType.DMA((3,)),
        ],
        compiler_params=pltpu.CompilerParams(vmem_limit_bytes=16 * 2**20),
        name="gather_rows",
    )(rows, near, far, extra)


def start_copies(pairs, sems):
    copies = [pltpu.make_async_copy(a, b, sems.at[i]) for i, (a, b) in enumerate(pairs)]
    for copy in copies:
        copy.start()
    return copies


def in_hbm(*values):
    return [pltpu.with_memory_space_constraint(value, pltpu.HBM) for value in values]


def forward_kernel(near, *rest):
    sources, (x_out, part, part16, table, picked, *copied, sems) = rest[:5], rest[5:]
    copies = start_copies(zip(sources, copied), sems)
    rows, far, upstream, v_proj, u_proj, staged = copied
    sent = []
    half, lanes = near.shape
    rank = v_proj.shape[0]
    table[:half] = near[...].astype(jnp.float32)
    copies[1].wait()
    table[half:] = far[...].astype(jnp.float32)
    copies[0].wait()
    pick_rows(rows, table, picked)
    for copy in copies[2:]:
        copy.wait()
    h_sum = jnp.zeros((rank, lanes), jnp.float32)
    d_sum = jnp.zeros((rank, lanes), jnp.float32)
    for k in range(half // CHUNK):
        here = slice(k * CHUNK, (k + 1) * CHUNK)
        x = picked[here, :]
        scaled = upstream[here, :].astype(jnp.float32) * x
        x16 = x.astype(jnp.bfloat16)
        staged[here, :] = x16
        sent.append(pltpu.make_async_copy(staged.at[here], x_out.at[here], sems.at[5 + k]))
        sent[-1].start()
        h_sum += jnp.dot(v_proj[:, here], x16, preferred_element_type=jnp.float32)
        d_sum += jnp.dot(
            u_proj[:, here], scaled.astype(jnp.bfloat16), preferred_element_type=jnp.float32
        )
    part[:rank] = h_sum
    part[rank:] = d_sum
    part16[:rank] = h_sum.astype(jnp.bfloat16)
    part16[rank:] = d_sum.astype(jnp.bfloat16)
    for copy in sent:
        copy.wait()


def ranks_kernel(part, other, ranks, message, total):
    rows = other.shape[0]
    value = part[...] + other[...].astype(jnp.float32)
    ranks[...] = value.astype(jnp.bfloat16)
    total[...] = value
    step = rows // 2 // 128
    for i in range(2):
        for j in range(step):
            to = i * rows // 2 + j * 128
            rank_rows = total[pl.ds(i * rows // 2 + j, 128, stride=step), :]
            message[to : to + 128, :] = rank_rows.astype(jnp.bfloat16)


def join_kernel(*rest):
    *blocks, message = rest
    rows = blocks[0].shape[0]
    for k, block in enumerate(blocks):
        message[k * rows : (k + 1) * rows, :] = block[...]


def join_blocks(blocks):
    rows, lanes = blocks[0].shape
    shape = jax.ShapeDtypeStruct((rows * len(blocks), lanes), blocks[0].dtype)
    return local_call(join_kernel, shape, *blocks, mib=6)


def grads_kernel(place, x_group, up_group, near_ranks, far_ranks, pieces, result, spread):
    count, wide, lanes = x_group.shape
    ny = count // 2
    y, c = place[0], place[1]
    both = near_ranks.shape[0] // ny
    ones = jnp.ones((8, 3 * lanes), jnp.bfloat16)
    sums = jnp.zeros((8, wide), jnp.float32)
    rank = both // 2
    for part in range(2):
        acc = jnp.zeros((rank, wide), jnp.float32)
        for k in range(ny):
            here = slice(k * both + part * rank, k * both + (part + 1) * rank)
            pair = lax.rem(y + ny - k, ny) * 2
            left = jnp.concatenate([near_ranks[here, :], far_ranks[here, :]], axis=1)
            right = [x_group[pair + c], x_group[pair + 1 - c]]
            if part == 0:
                ups = [up_group[pair + c], up_group[pair + 1 - c]]
                scaled = [up.astype(jnp.float32) * x.astype(jnp.float32) for up, x in zip(ups, right)]
                for value in scaled:
                    sums = sums + dot_last(ones, jnp.concatenate(split3(value), axis=1))
                right = [value.astype(jnp.bfloat16) for value in scaled]
            acc = acc + dot_last(left, jnp.concatenate(right, axis=1))
        result[:, part * wide : (part + 1) * wide] = acc
    dests, height, _ = pieces.shape
    blocks = 2 * wide // lanes
    for j in range(rank // dests):
        for k in range(blocks):
            spread[pl.ds(j * blocks + k, dests, stride=height), :] = result[
                j * dests : (j + 1) * dests, k * lanes : (k + 1) * lanes
            ]
    first = rank // dests * blocks
    for k in range(wide // lanes):
        row = sums[:1, k * lanes : (k + 1) * lanes]
        high = row.astype(jnp.bfloat16).astype(jnp.float32)
        for i, value in enumerate((high, row - high)):
            at = first + i * (wide // lanes) + k
            spread[pl.ds(at, dests, stride=height), :] = jnp.broadcast_to(value, (dests, lanes))
    pieces[...] = spread[...].reshape(dests, height, lanes).astype(jnp.bfloat16)


def arrive_kernel(got, d_looked, grad_u, grad_v, grad_bias, *, block, wide, norm):
    sources, height, lanes = got.shape
    for k in range(sources):
        d_looked[:, k * lanes : (k + 1) * lanes] = got[k, :block, :]
    columns = wide // lanes
    group = grad_u.shape[1] // wide
    first = 2 * columns * grad_u.shape[0]
    for b in range(group):
        total = jnp.zeros((height - block, lanes), jnp.float32)
        for k in range(sources // group):
            total += got[k * group + b, block:, :].astype(jnp.float32)
        total = total * norm
        for k in range(columns):
            here = slice(b * wide + k * lanes, b * wide + (k + 1) * lanes)
            for j in range(grad_u.shape[0]):
                row = j * 2 * columns + k
                grad_u[j : j + 1, here] = total[row : row + 1]
                grad_v[j : j + 1, here] = total[row + columns : row + columns + 1]
            row = first + k
            grad_bias[b * columns + k : b * columns + k + 1, :] = (
                total[row : row + 1] + total[row + columns : row + columns + 1]
            )


def inverse_rows(column_owner, first_column, count):
    wires = jnp.arange(column_owner.shape[0], dtype=jnp.int32)
    high = column_owner // 128 - first_column // 128
    low = column_owner % 128
    pick = (high[None, :] == jnp.arange(count // 128, dtype=jnp.int32)[:, None]).astype(jnp.bfloat16)
    lanes = low[:, None] == jnp.arange(128, dtype=jnp.int32)[None, :]
    values = jnp.concatenate(
        [
            jnp.where(lanes, (wires // 128)[:, None].astype(jnp.bfloat16), 0),
            jnp.where(lanes, (wires % 128)[:, None].astype(jnp.bfloat16), 0),
        ],
        axis=1,
    )
    found = jnp.dot(pick, values, preferred_element_type=jnp.float32).astype(jnp.int32)
    return (found[:, :128] * 128 + found[:, 128:]).reshape(-1)


def step(looked, column_owner, v_proj, u_proj, bias, upstream):
    y, c, t = (lax.axis_index(a).astype(jnp.int32) for a in ("y", "c", "t"))
    ny = lax.axis_size("y")
    dp_count = lax.axis_size(DP)
    block_rows = looked.shape[0]
    rank, half_width = v_proj.shape
    samples = upstream.shape[1]
    norm = 1.0 / math.sqrt(samples * dp_count)
    bf16 = jnp.bfloat16

    array = jax.ShapeDtypeStruct
    group = 2 * ny
    wide = half_width // group
    arrived = lax.all_to_all(looked, DP, split_axis=1, concat_axis=0, tiled=True)
    partner = lax.ppermute(arrived, "t", SWAP)
    up_group = lax.all_to_all(
        upstream.reshape(group, wide, samples), ("y", "c"), split_axis=0, concat_axis=0, tiled=True
    )
    wire = inverse_rows(column_owner, t * half_width, half_width)
    side = wire // block_rows % 2
    spot = wire // (2 * block_rows) * block_rows + wire % block_rows
    x_rows = jnp.where(side == t, 0, half_width) + spot
    x_zero, part, part16 = local_call(
        forward_kernel,
        [
            array((half_width, samples), bf16),
            array((2 * rank, samples), jnp.float32),
            array((2 * rank, samples), bf16),
        ],
        arrived,
        *in_hbm(x_rows, partner, upstream, v_proj, u_proj),
        scratch_shapes=[
            pltpu.VMEM((2 * half_width, samples), jnp.float32),
            pltpu.VMEM((half_width, samples), jnp.float32),
            pltpu.SMEM(x_rows.shape, jnp.int32),
            pltpu.VMEM(partner.shape, bf16),
            pltpu.VMEM(upstream.shape, bf16),
            pltpu.VMEM(v_proj.shape, bf16),
            pltpu.VMEM(u_proj.shape, bf16),
            pltpu.VMEM(upstream.shape, bf16),
            pltpu.SemaphoreType.DMA((5 + half_width // CHUNK,)),
        ],
        specs=[VMEM] + [HBM] * 5,
        outs=[HBM, VMEM, VMEM],
        input_output_aliases={2: 0},
        mib=28,
    )
    other = lax.ppermute(part16, "t", SWAP)
    x_group = lax.all_to_all(
        x_zero.reshape(group, wide, samples), ("y", "c"), split_axis=0, concat_axis=0, tiled=True
    )
    ranks, message = local_call(
        ranks_kernel,
        [array((2 * rank, samples), bf16)] * 2,
        part,
        other,
        scratch_shapes=[pltpu.VMEM((2 * rank, samples), jnp.float32)],
        mib=4,
    )

    mix = dot_first(u_proj, ranks[:rank]) + bias[:, None]
    cotan = upstream.astype(jnp.float32)
    dx_zero = (cotan * (mix + 1.0) + dot_first(v_proj, ranks[rank:])).astype(bf16)
    dx_other = lax.ppermute(dx_zero, "t", SWAP)

    blocks = [message]
    for k in range(1, ny):
        blocks.append(shift(blocks[0], "y", ny, k))
    near_ranks = join_blocks(blocks)
    far_ranks = lax.ppermute(near_ranks, "c", SWAP)
    height = rank // dp_count * (2 * wide // 128) + 2 * wide // 128
    pieces = local_call(
        grads_kernel,
        array((dp_count, height, 128), bf16),
        jnp.stack([y, c]),
        x_group,
        up_group,
        near_ranks,
        far_ranks,
        scalars=1,
        scratch_shapes=[
            pltpu.VMEM((rank, 2 * wide), jnp.float32),
            pltpu.VMEM((dp_count * height, 128), jnp.float32),
        ],
        mib=16,
    )

    columns = lax.dynamic_index_in_dim(
        column_owner.reshape(dp_count, 2, block_rows), t, 1, keepdims=False
    ).reshape(-1)
    out_rows = jnp.where(columns // half_width == t, 0, half_width) + columns % half_width
    outgoing = gather(out_rows, dx_zero, dx_other, pieces)
    got = lax.all_to_all(outgoing, DP, split_axis=0, concat_axis=0, tiled=True)
    d_looked, grad_u, grad_v, grad_bias = local_call(
        lambda *refs: arrive_kernel(*refs, block=block_rows, wide=wide, norm=norm),
        [
            array((block_rows, dp_count * samples), bf16),
            array((rank // dp_count, half_width), jnp.float32),
            array((rank // dp_count, half_width), jnp.float32),
            array((half_width // 128, 128), jnp.float32),
        ],
        got,
        mib=8,
    )
    return (d_looked, grad_u, grad_v, grad_bias.reshape(-1))


def solution(mesh):
    fine = Mesh(mesh.devices.reshape(8, 2, 4, 2, 2), DP + ("t",))
    in_specs = (
        P(DP + ("t",), None),
        P(),
        P(None, "t"),
        P(None, "t"),
        P("t"),
        P("t", DP),
    )
    out_specs = (P(DP + ("t",), None), P(DP, "t"), P(DP, "t"), P("t"))
    return jax.shard_map(step, mesh=fine, in_specs=in_specs, out_specs=out_specs, check_vma=False)
```

```python
import math

import jax
import jax.numpy as jnp
from jax import lax
from jax.experimental import pallas as pl
from jax.experimental.pallas import tpu as pltpu
from jax.sharding import Mesh, PartitionSpec as P


DP = ("z", "xl", "y", "c")
SWAP = [(0, 1), (1, 0)]
UNROLL = 64
CHUNK = 512


SMEM = pl.BlockSpec(memory_space=pltpu.SMEM)
VMEM = pl.BlockSpec(memory_space=pltpu.VMEM)
HBM = pl.BlockSpec(memory_space=pltpu.HBM)


def dot_last(left, right):
    return lax.dot_general(
        left, right, (((1,), (1,)), ((), ())), preferred_element_type=jnp.float32
    )


def dot_first(left, right):
    return lax.dot_general(
        left, right, (((0,), (0,)), ((), ())), preferred_element_type=jnp.float32
    )


def shift(value, axis, size, by):
    return lax.ppermute(value, axis, [(i, (i + by) % size) for i in range(size)])


def split3(value):
    high = value.astype(jnp.bfloat16)
    rest = value - high.astype(jnp.float32)
    middle = rest.astype(jnp.bfloat16)
    low = (rest - middle.astype(jnp.float32)).astype(jnp.bfloat16)
    return high, middle, low


def local_call(body, out_shape, *args, scalars=0, mib, specs=None, outs=None, **kwargs):
    return pl.pallas_call(
        body,
        out_shape=out_shape,
        in_specs=specs or [SMEM] * scalars + [VMEM] * (len(args) - scalars),
        out_specs=outs or jax.tree.map(lambda _: VMEM, out_shape),
        compiler_params=pltpu.CompilerParams(vmem_limit_bytes=mib * 2**20),
        **kwargs,
    )(*args)


def pick_rows(rows, table, picked):
    def step(i, carry):
        for j in range(UNROLL):
            k = i * UNROLL + j
            picked[pl.ds(k, 1), :] = table[pl.ds(rows[k], 1), :]
        return carry

    lax.fori_loop(0, picked.shape[0] // UNROLL, step, 0)


def gather_kernel(rows_in, near, far_in, extra, out, rows, far, table, picked, sems):
    half = near.shape[0]
    dests, height, lanes = out.shape
    block = height - extra.shape[1]
    copies = start_copies(((far_in, far), (rows_in, rows), (extra, out.at[:, block:, :])), sems)
    table[:half] = near[...].astype(jnp.float32)
    copies[0].wait()
    table[half:] = far[...].astype(jnp.float32)
    copies[1].wait()
    pick_rows(rows, table, picked)
    out[:, :block, :] = picked[...].reshape(dests, block, lanes).astype(out.dtype)
    copies[2].wait()


def gather(rows, near, far, extra):
    count, lanes = rows.shape[0], near.shape[1]
    dests, height, _ = extra.shape
    rows, far = in_hbm(rows, far)
    return pl.pallas_call(
        gather_kernel,
        out_shape=jax.ShapeDtypeStruct((dests, count // dests + height, lanes), near.dtype),
        in_specs=[HBM, VMEM, HBM, VMEM],
        out_specs=VMEM,
        scratch_shapes=[
            pltpu.SMEM((count,), jnp.int32),
            pltpu.VMEM(near.shape, near.dtype),
            pltpu.VMEM((2 * near.shape[0], lanes), jnp.float32),
            pltpu.VMEM((count, lanes), jnp.float32),
            pltpu.SemaphoreType.DMA((3,)),
        ],
        compiler_params=pltpu.CompilerParams(vmem_limit_bytes=16 * 2**20),
        name="gather_rows",
    )(rows, near, far, extra)


def start_copies(pairs, sems):
    copies = [pltpu.make_async_copy(a, b, sems.at[i]) for i, (a, b) in enumerate(pairs)]
    for copy in copies:
        copy.start()
    return copies


def in_hbm(*values):
    return [pltpu.with_memory_space_constraint(value, pltpu.HBM) for value in values]


def forward_kernel(near, *rest):
    sources, (x_out, part, part16, table, picked, *copied, sems) = rest[:5], rest[5:]
    copies = start_copies(zip(sources, copied), sems)
    rows, far, upstream, v_proj, u_proj, staged = copied
    sent = []
    half, lanes = near.shape
    rank = v_proj.shape[0]
    table[:half] = near[...].astype(jnp.float32)
    copies[1].wait()
    table[half:] = far[...].astype(jnp.float32)
    copies[0].wait()
    pick_rows(rows, table, picked)
    for k in range(half // CHUNK):
        here = slice(k * CHUNK, (k + 1) * CHUNK)
        staged[here, :] = picked[here, :].astype(jnp.bfloat16)
        sent.append(pltpu.make_async_copy(staged.at[here], x_out.at[here], sems.at[5 + k]))
        sent[-1].start()
    for copy in copies[2:]:
        copy.wait()
    h_sum = jnp.zeros((rank, lanes), jnp.float32)
    d_sum = jnp.zeros((rank, lanes), jnp.float32)
    for k in range(half // CHUNK):
        here = slice(k * CHUNK, (k + 1) * CHUNK)
        x = picked[here, :]
        scaled = upstream[here, :].astype(jnp.float32) * x
        x16 = x.astype(jnp.bfloat16)
        h_sum += jnp.dot(v_proj[:, here], x16, preferred_element_type=jnp.float32)
        d_sum += jnp.dot(
            u_proj[:, here], scaled.astype(jnp.bfloat16), preferred_element_type=jnp.float32
        )
    part[:rank] = h_sum
    part[rank:] = d_sum
    part16[:rank] = h_sum.astype(jnp.bfloat16)
    part16[rank:] = d_sum.astype(jnp.bfloat16)
    for copy in sent:
        copy.wait()


def ranks_kernel(part, other, ranks, message, total):
    rows = other.shape[0]
    value = part[...] + other[...].astype(jnp.float32)
    ranks[...] = value.astype(jnp.bfloat16)
    total[...] = value
    step = rows // 2 // 128
    for i in range(2):
        for j in range(step):
            to = i * rows // 2 + j * 128
            rank_rows = total[pl.ds(i * rows // 2 + j, 128, stride=step), :]
            message[to : to + 128, :] = rank_rows.astype(jnp.bfloat16)


def join_kernel(*rest):
    *blocks, message = rest
    rows = blocks[0].shape[0]
    for k, block in enumerate(blocks):
        message[k * rows : (k + 1) * rows, :] = block[...]


def join_blocks(blocks):
    rows, lanes = blocks[0].shape
    shape = jax.ShapeDtypeStruct((rows * len(blocks), lanes), blocks[0].dtype)
    return local_call(join_kernel, shape, *blocks, mib=6)


def grads_kernel(place, x_group, up_group, near_ranks, far_ranks, pieces, result, spread):
    count, wide, lanes = x_group.shape
    ny = count // 2
    y, c = place[0], place[1]
    both = near_ranks.shape[0] // ny
    ones = jnp.ones((8, 3 * lanes), jnp.bfloat16)
    sums = jnp.zeros((8, wide), jnp.float32)
    rank = both // 2
    for part in range(2):
        acc = jnp.zeros((rank, wide), jnp.float32)
        for k in range(ny):
            here = slice(k * both + part * rank, k * both + (part + 1) * rank)
            pair = lax.rem(y + ny - k, ny) * 2
            left = jnp.concatenate([near_ranks[here, :], far_ranks[here, :]], axis=1)
            right = [x_group[pair + c], x_group[pair + 1 - c]]
            if part == 0:
                ups = [up_group[pair + c], up_group[pair + 1 - c]]
                scaled = [up.astype(jnp.float32) * x.astype(jnp.float32) for up, x in zip(ups, right)]
                for value in scaled:
                    sums = sums + dot_last(ones, jnp.concatenate(split3(value), axis=1))
                right = [value.astype(jnp.bfloat16) for value in scaled]
            acc = acc + dot_last(left, jnp.concatenate(right, axis=1))
        result[:, part * wide : (part + 1) * wide] = acc
    dests, height, _ = pieces.shape
    blocks = 2 * wide // lanes
    for j in range(rank // dests):
        for k in range(blocks):
            spread[pl.ds(j * blocks + k, dests, stride=height), :] = result[
                j * dests : (j + 1) * dests, k * lanes : (k + 1) * lanes
            ]
    first = rank // dests * blocks
    for k in range(wide // lanes):
        row = sums[:1, k * lanes : (k + 1) * lanes]
        high = row.astype(jnp.bfloat16).astype(jnp.float32)
        for i, value in enumerate((high, row - high)):
            at = first + i * (wide // lanes) + k
            spread[pl.ds(at, dests, stride=height), :] = jnp.broadcast_to(value, (dests, lanes))
    pieces[...] = spread[...].reshape(dests, height, lanes).astype(jnp.bfloat16)


def arrive_kernel(got, d_looked, grad_u, grad_v, grad_bias, *, block, wide, norm):
    sources, height, lanes = got.shape
    for k in range(sources):
        d_looked[:, k * lanes : (k + 1) * lanes] = got[k, :block, :]
    columns = wide // lanes
    group = grad_u.shape[1] // wide
    first = 2 * columns * grad_u.shape[0]
    for b in range(group):
        total = jnp.zeros((height - block, lanes), jnp.float32)
        for k in range(sources // group):
            total += got[k * group + b, block:, :].astype(jnp.float32)
        total = total * norm
        for k in range(columns):
            here = slice(b * wide + k * lanes, b * wide + (k + 1) * lanes)
            for j in range(grad_u.shape[0]):
                row = j * 2 * columns + k
                grad_u[j : j + 1, here] = total[row : row + 1]
                grad_v[j : j + 1, here] = total[row + columns : row + columns + 1]
            row = first + k
            grad_bias[b * columns + k : b * columns + k + 1, :] = (
                total[row : row + 1] + total[row + columns : row + columns + 1]
            )


def inverse_rows(column_owner, first_column, count):
    wires = jnp.arange(column_owner.shape[0], dtype=jnp.int32)
    high = column_owner // 128 - first_column // 128
    low = column_owner % 128
    pick = (high[None, :] == jnp.arange(count // 128, dtype=jnp.int32)[:, None]).astype(jnp.bfloat16)
    lanes = low[:, None] == jnp.arange(128, dtype=jnp.int32)[None, :]
    values = jnp.concatenate(
        [
            jnp.where(lanes, (wires // 128)[:, None].astype(jnp.bfloat16), 0),
            jnp.where(lanes, (wires % 128)[:, None].astype(jnp.bfloat16), 0),
        ],
        axis=1,
    )
    found = jnp.dot(pick, values, preferred_element_type=jnp.float32).astype(jnp.int32)
    return (found[:, :128] * 128 + found[:, 128:]).reshape(-1)


def step(looked, column_owner, v_proj, u_proj, bias, upstream):
    y, c, t = (lax.axis_index(a).astype(jnp.int32) for a in ("y", "c", "t"))
    ny = lax.axis_size("y")
    dp_count = lax.axis_size(DP)
    block_rows = looked.shape[0]
    rank, half_width = v_proj.shape
    samples = upstream.shape[1]
    norm = 1.0 / math.sqrt(samples * dp_count)
    bf16 = jnp.bfloat16

    array = jax.ShapeDtypeStruct
    group = 2 * ny
    wide = half_width // group
    arrived = lax.all_to_all(looked, DP, split_axis=1, concat_axis=0, tiled=True)
    partner = lax.ppermute(arrived, "t", SWAP)
    up_group = lax.all_to_all(
        upstream.reshape(group, wide, samples), ("y", "c"), split_axis=0, concat_axis=0, tiled=True
    )
    wire = inverse_rows(column_owner, t * half_width, half_width)
    side = wire // block_rows % 2
    spot = wire // (2 * block_rows) * block_rows + wire % block_rows
    x_rows = jnp.where(side == t, 0, half_width) + spot
    x_zero, part, part16 = local_call(
        forward_kernel,
        [
            array((half_width, samples), bf16),
            array((2 * rank, samples), jnp.float32),
            array((2 * rank, samples), bf16),
        ],
        arrived,
        *in_hbm(x_rows, partner, upstream, v_proj, u_proj),
        scratch_shapes=[
            pltpu.VMEM((2 * half_width, samples), jnp.float32),
            pltpu.VMEM((half_width, samples), jnp.float32),
            pltpu.SMEM(x_rows.shape, jnp.int32),
            pltpu.VMEM(partner.shape, bf16),
            pltpu.VMEM(upstream.shape, bf16),
            pltpu.VMEM(v_proj.shape, bf16),
            pltpu.VMEM(u_proj.shape, bf16),
            pltpu.VMEM(upstream.shape, bf16),
            pltpu.SemaphoreType.DMA((5 + half_width // CHUNK,)),
        ],
        specs=[VMEM] + [HBM] * 5,
        outs=[HBM, VMEM, VMEM],
        input_output_aliases={2: 0},
        mib=28,
    )
    other = lax.ppermute(part16, "t", SWAP)
    x_group = lax.all_to_all(
        x_zero.reshape(group, wide, samples), ("y", "c"), split_axis=0, concat_axis=0, tiled=True
    )
    ranks, message = local_call(
        ranks_kernel,
        [array((2 * rank, samples), bf16)] * 2,
        part,
        other,
        scratch_shapes=[pltpu.VMEM((2 * rank, samples), jnp.float32)],
        mib=4,
    )

    mix = dot_first(u_proj, ranks[:rank]) + bias[:, None]
    cotan = upstream.astype(jnp.float32)
    dx_zero = (cotan * (mix + 1.0) + dot_first(v_proj, ranks[rank:])).astype(bf16)
    dx_other = lax.ppermute(dx_zero, "t", SWAP)

    blocks = [message]
    for k in range(1, ny):
        blocks.append(shift(blocks[0], "y", ny, k))
    near_ranks = join_blocks(blocks)
    far_ranks = lax.ppermute(near_ranks, "c", SWAP)
    height = rank // dp_count * (2 * wide // 128) + 2 * wide // 128
    pieces = local_call(
        grads_kernel,
        array((dp_count, height, 128), bf16),
        jnp.stack([y, c]),
        x_group,
        up_group,
        near_ranks,
        far_ranks,
        scalars=1,
        scratch_shapes=[
            pltpu.VMEM((rank, 2 * wide), jnp.float32),
            pltpu.VMEM((dp_count * height, 128), jnp.float32),
        ],
        mib=16,
    )

    columns = lax.dynamic_index_in_dim(
        column_owner.reshape(dp_count, 2, block_rows), t, 1, keepdims=False
    ).reshape(-1)
    out_rows = jnp.where(columns // half_width == t, 0, half_width) + columns % half_width
    outgoing = gather(out_rows, dx_zero, dx_other, pieces)
    got = lax.all_to_all(outgoing, DP, split_axis=0, concat_axis=0, tiled=True)
    d_looked, grad_u, grad_v, grad_bias = local_call(
        lambda *refs: arrive_kernel(*refs, block=block_rows, wide=wide, norm=norm),
        [
            array((block_rows, dp_count * samples), bf16),
            array((rank // dp_count, half_width), jnp.float32),
            array((rank // dp_count, half_width), jnp.float32),
            array((half_width // 128, 128), jnp.float32),
        ],
        got,
        mib=8,
    )
    return (d_looked, grad_u, grad_v, grad_bias.reshape(-1))


def solution(mesh):
    fine = Mesh(mesh.devices.reshape(8, 2, 4, 2, 2), DP + ("t",))
    in_specs = (
        P(DP + ("t",), None),
        P(),
        P(None, "t"),
        P(None, "t"),
        P("t"),
        P("t", DP),
    )
    out_specs = (P(DP + ("t",), None), P(DP, "t"), P(DP, "t"), P("t"))
    return jax.shard_map(step, mesh=fine, in_specs=in_specs, out_specs=out_specs, check_vma=False)
```
